32 devices in a mesh: ctx: 4 (over x, core), dp: 2 (over y), tp: 4 (over z).
Axes of the slice: x: 2, y: 2, z: 4, core: 2. Of those that a mesh axis runs over, the one named last changes fastest.
Arguments:
- token_ids: int32 [4, 4], replicated, may hold values from 0 to 50279
- decode_prompt: int32 [4], replicated, may hold values from 0 to 3, as said below
- embedding: bfloat16 [50280, 4096], P('dp', ('ctx', 'tp')), may hold values from -6 to 6
- norm_gain: float32 [4096], replicated, may hold values from 0.1 to 1.9
- w_zx: bfloat16 [2, 128, 64, 4096], P(None, ('tp', 'ctx')), may hold values from -0.09375 to 0.09375
- w_bcdt: bfloat16 [4096, 384], P(None, ('ctx', 'tp')), may hold values from -0.09375 to 0.09375
- conv_x_weight: float32 [4, 128, 64], P(None, ('tp', 'ctx')), may hold values from -3 to 3
- conv_x_bias: float32 [128, 64], P(('tp', 'ctx')), may hold values from -3 to 3
- conv_bc_weight: float32 [4, 256], replicated, may hold values from -3 to 3
- conv_bc_bias: float32 [256], replicated, may hold values from -3 to 3
- dt_bias: float32 [128], P(('tp', 'ctx')), may hold values from -4 to -1
- a_log: float32 [128], P(('tp', 'ctx')), may hold values from 0 to 2.7
- d_skip: float32 [128], P(('tp', 'ctx')), may hold values from 0.5 to 1.5
- gate_norm_gain: float32 [128, 64], P(('tp', 'ctx')), may hold values from 0.1 to 1.9
- w_out: bfloat16 [128, 64, 4096], P(('tp', 'ctx')), may hold values from -0.0625 to 0.0625
- state_parts: bfloat16 [4, 4, 128, 64, 128], P('ctx', 'dp', 'tp'), may hold values from -6 to 6
- seg_rate: float32 [4, 4, 128], P('ctx', 'dp', 'tp'), may hold values from 0 to 4
- x_tail: bfloat16 [4, 3, 128, 64], P('dp', None, ('tp', 'ctx')), may hold values from -6 to 6
- bc_tail: bfloat16 [4, 3, 256], P('dp'), may hold values from -6 to 6
Outputs:
- mixer_out: bfloat16 [4, 4, 4096], P(None, 'dp', ('ctx', 'tp'))
- final_state: float32 [4, 128, 64, 128], P('dp', ('tp', 'ctx'))
The draws below stay inside these ranges and needn't reach their ends.
Inputs may be any that keep to these rules, and one draw needn't show every extreme that they name: decode_prompt is a permutation of the prompts; slot s is decoded by dp group s // 2, and prompt q is held by dp group q // 2; the 2 prompts held by one dp group are decoded by 2 different dp groups.
All inputs are finite; a program needn't handle non-finite values.
Results may differ from the reference program's by a relative error of at most 0.02.
Values may be sent and summed in bfloat16 or wider, within the bound.
A program may use at most 64 MiB of HBM per device.

```python
import math
import jax
import jax.numpy as jnp
import numpy as np
from jax import lax

D = 4096
HEADS = 128
HEAD_DIM = 64
STATE = 128
VOCAB = 50280
CONV = 4
STEPS = 4
PR_DEV = 2
PROMPTS = 4
PREFILL_SEGMENTS = 4
N_DP = 2


def draw_decode_prompt(key, part):
    base = jax.random.fold_in(key, 11)
    key_label, key_offset, key_link, key_slot = jax.random.split(base, 4)
    label = jax.random.permutation(key_label, N_DP).astype(jnp.int32)
    owner = jnp.argsort(label).astype(jnp.int32)
    offsets = jax.random.permutation(key_offset, N_DP)[:PR_DEV].astype(jnp.int32)
    link_prompt = jax.vmap(lambda single: jax.random.permutation(single, PR_DEV))(jax.random.split(key_link, N_DP)).astype(jnp.int32)
    slot_order = jax.vmap(lambda single: jax.random.permutation(single, PR_DEV))(jax.random.split(key_slot, N_DP)).astype(jnp.int32)
    source = owner[(label[:, None] - offsets[None, :]) % N_DP]
    links = jnp.arange(PR_DEV, dtype=jnp.int32)[None, :]
    prompt = source * PR_DEV + link_prompt[source, links]
    slots = jnp.arange(N_DP, dtype=jnp.int32)[:, None] * PR_DEV + slot_order
    return jnp.zeros((N_DP * PR_DEV,), jnp.int32).at[slots.reshape(-1)].set(prompt.reshape(-1).astype(jnp.int32))


def draw_seg_rate(key, part):
    root_random_key = jax.random.fold_in(key, 23)
    plateau_random_key, quick_random_key, choose_random_key, jitter_random_key, spike_random_key, length_random_key = jax.random.split(root_random_key, 6)
    leading = (PROMPTS, HEADS)
    complete_shape = (PREFILL_SEGMENTS, PROMPTS, HEADS)
    slow_low, slow_high, fast_share, rough_low, rough_high = (0.1, 1.5, 0.25, 0.5, 1.5)
    slow_rate = jnp.exp(jax.random.uniform(plateau_random_key, leading, jnp.float32, math.log(slow_low), math.log(slow_high)))
    fast_rate = jnp.exp(jax.random.uniform(quick_random_key, leading, jnp.float32, math.log(2.0), math.log(5.0)))
    chosen = jax.random.uniform(choose_random_key, leading, jnp.float32) < fast_share
    plateau_rate = jnp.where(chosen, fast_rate, slow_rate) / PREFILL_SEGMENTS
    jitter_amount = jax.random.uniform(jitter_random_key, complete_shape, jnp.float32, rough_low, rough_high)
    spike_events = jax.random.uniform(spike_random_key, complete_shape, jnp.float32) < 1.0 / PREFILL_SEGMENTS
    spike_length = jax.random.uniform(length_random_key, complete_shape, jnp.float32, 0.22, 0.69)
    return (plateau_rate[None] * jitter_amount + jnp.where(spike_events, spike_length, 0.0)).astype(jnp.float32)


def touch_ends(drawn, stream_key, least, largest):
    index_at = [jax.random.randint(jax.random.fold_in(stream_key, axis), (), 0, length) for axis, length in enumerate(drawn.shape)]
    main_axis = drawn.shape.index(max(drawn.shape))
    beside = index_at[:main_axis] + [(index_at[main_axis] + 1) % drawn.shape[main_axis]] + index_at[main_axis + 1:]
    return drawn.at[tuple(index_at)].set(least).at[tuple(beside)].set(largest)


def spiked(result, key, source, target, parts, factor):
    owner, partner = [(jnp.arange(result.shape[axis_at]) // (result.shape[axis_at] // parts)).reshape([-1 if axis == axis_at else 1 for axis in range(result.ndim)]) for axis_at in (source, target)]
    chosen = jax.random.permutation(key, parts)[partner]
    strong = (owner == chosen) | (owner == (partner + parts // 2) % parts)
    return jnp.where(strong, factor * result, result)


def levels(key, extent, cuts, low, largest):
    level = 1.0
    for axis_at, parts in cuts:
        steps = jax.random.uniform(jax.random.fold_in(jax.random.fold_in(key, 6), axis_at), (parts,), jnp.float32, low / len(cuts), largest / len(cuts))
        level = level * jnp.repeat(jnp.exp(steps), extent[axis_at] // parts).reshape((-1,) + (1,) * (len(extent) - 1 - axis_at))
    return level


def rank_bounds(number_of, skew):
    weights = [(1 << 20) // math.isqrt(grade ** skew) + 1 for grade in range(1, number_of + 1)]
    width = 1 + sum(weights) // (1 << 30)
    return np.cumsum(np.array([max(1, weight // width) for weight in weights]))


def ranked_ids(stream_key, shape, amount, skew):
    listing = rank_bounds(amount, skew)
    pick = jax.random.randint(jax.random.fold_in(stream_key, 1), shape, 0, int(listing[amount - 1]))
    rank = jnp.searchsorted(jnp.asarray(listing, jnp.int32), pick, side="right")
    return jax.random.permutation(jax.random.fold_in(stream_key, 2), amount)[rank].astype(jnp.int32)


def gaussian(rng, shape, scale, most, pieces=(), kind=jnp.bfloat16):
    drawn = scale * jax.random.normal(rng, shape, jnp.float32)
    if pieces:
        drawn = drawn * levels(rng, shape, pieces, -0.22, 0.18)
    return jnp.clip(drawn, -most, most).astype(kind)


def gaussian_with(stream_key, dims, width, limit, shards, heavy, kind=jnp.bfloat16):
    entries = width * jax.random.normal(stream_key, dims, jnp.float32)
    if shards:
        entries = entries * levels(stream_key, dims, shards, -0.22, 0.18)
    return jnp.clip(spiked(entries, jax.random.fold_in(stream_key, 3), *heavy), -limit, limit).astype(kind)


def setup_inputs(seed: int = 0) -> dict:
    key_list = jax.random.split(jax.random.key(seed), 20)
    return {
        "token_ids": touch_ends(ranked_ids(key_list[0], (STEPS, PROMPTS), VOCAB, 2), jax.random.fold_in(key_list[0], 3), 0, VOCAB - 1).astype(jnp.int32),
        "decode_prompt": draw_decode_prompt(jax.random.fold_in(key_list[19], 71), 0),
        "embedding": gaussian(key_list[2], (VOCAB, D), 1.0, 6.0, ((0, 2), (1, 16))),
        "norm_gain": jnp.clip(1.0 + 0.18 * jax.random.normal(key_list[3], (D,), jnp.float32), 0.1, 1.9),
        "w_zx": gaussian(key_list[4], (2, HEADS, HEAD_DIM, D), D ** -0.5, 0.09375, ((1, 16),)),
        "w_bcdt": gaussian(key_list[5], (D, 2 * STATE + HEADS), D ** -0.5, 0.09375, ((1, 16),)),
        "conv_x_weight": gaussian(key_list[6], (CONV, HEADS, HEAD_DIM), CONV ** -0.5, 3.0, ((1, 16),), jnp.float32),
        "conv_x_bias": gaussian(key_list[7], (HEADS, HEAD_DIM), 0.5, 3.0, ((0, 16),), jnp.float32),
        "conv_bc_weight": gaussian(key_list[8], (CONV, 2 * STATE), CONV ** -0.5, 3.0, (), jnp.float32),
        "conv_bc_bias": gaussian(key_list[9], (2 * STATE,), 0.5, 3.0, (), jnp.float32),
        "dt_bias": jnp.clip(-4.0 + 3.0 * jax.random.uniform(key_list[10], (HEADS,), jnp.float32) ** levels(key_list[10], (HEADS,), ((0, 16),), -0.2, 0.2), -4.0, -1.0),
        "a_log": jnp.clip(2.7 * jax.random.uniform(key_list[11], (HEADS,), jnp.float32) ** levels(key_list[11], (HEADS,), ((0, 16),), -0.2, 0.2), 0.0, 2.7),
        "d_skip": jnp.clip(0.5 + 1.0 * jax.random.uniform(key_list[12], (HEADS,), jnp.float32) ** levels(key_list[12], (HEADS,), ((0, 16),), -0.2, 0.2), 0.5, 1.5),
        "gate_norm_gain": jnp.clip(1.0 + 0.18 * jax.random.normal(key_list[13], (HEADS, HEAD_DIM), jnp.float32), 0.1, 1.9),
        "w_out": gaussian(key_list[14], (HEADS, HEAD_DIM, D), (HEADS * HEAD_DIM) ** -0.5, 0.0625, ((0, 16),)),
        "state_parts": gaussian_with(key_list[15], (PREFILL_SEGMENTS, PROMPTS, HEADS, HEAD_DIM, STATE), 1.0, 6.0, ((0, 4), (1, 2), (2, 4)), (0, 2, 4, 2.0)),
        "seg_rate": draw_seg_rate(jax.random.fold_in(key_list[19], 71), 0),
        "x_tail": gaussian(key_list[17], (PROMPTS, CONV - 1, HEADS, HEAD_DIM), 1.0, 6.0, ((0, 2), (2, 16))),
        "bc_tail": gaussian(key_list[18], (PROMPTS, CONV - 1, 2 * STATE), 1.0, 6.0, ((0, 2),)),
    }


epsilon = 1e-05

def rms_scale(values, gain):
    return values * lax.rsqrt(lax.optimization_barrier(jnp.mean(values * values, axis=-1, keepdims=True)) + epsilon) * gain

def reference(token_ids, decode_prompt, embedding, norm_gain, w_zx, w_bcdt, conv_x_weight, conv_x_bias, conv_bc_weight, conv_bc_bias, dt_bias, a_log, d_skip, gate_norm_gain, w_out, state_parts, seg_rate, x_tail, bc_tail):
    suffix = jnp.cumsum(seg_rate[::-1], axis=0)[::-1] - seg_rate
    seg_weight = jnp.exp(-suffix)

    def add_segment(running, seg_index):
        segment_part = lax.dynamic_index_in_dim(state_parts, seg_index, 0, keepdims=False).astype(jnp.float32)
        factor = lax.dynamic_index_in_dim(seg_weight, seg_index, 0, keepdims=False)
        scaled = (factor[:, :, None, None] * segment_part).astype(jnp.bfloat16)
        scaled = lax.optimization_barrier(scaled)
        return (running + scaled.astype(jnp.float32), None)
    combined, _ = lax.scan(add_segment, jnp.zeros(state_parts.shape[1:], jnp.float32), jnp.arange(PREFILL_SEGMENTS, dtype=jnp.int32))
    ssm_state = combined[decode_prompt]
    x_window = x_tail[decode_prompt].astype(jnp.float32)
    bc_window = bc_tail[decode_prompt].astype(jnp.float32)
    slot_tokens = token_ids[:, decode_prompt]
    embedded = embedding[slot_tokens]
    normed = rms_scale(embedded.astype(jnp.float32), norm_gain).astype(jnp.bfloat16)
    projected = jnp.einsum('tpd,khed->ktphe', normed.astype(jnp.float32), w_zx.astype(jnp.float32))
    columns = jnp.einsum('tpd,dc->tpc', normed.astype(jnp.float32), w_bcdt.astype(jnp.float32))
    decay_rate = -jnp.exp(a_log)
    gated_steps = []
    for moment in range(STEPS):
        x_window = jnp.concatenate([x_window, projected[1, moment][:, None]], axis=1)
        bc_window = jnp.concatenate([bc_window, columns[moment, :, None, :2 * STATE]], axis=1)
        x_conv = jax.nn.silu(jnp.einsum('pkhe,khe->phe', x_window, conv_x_weight) + conv_x_bias)
        bc_conv = jax.nn.silu(jnp.einsum('pkn,kn->pn', bc_window, conv_bc_weight) + conv_bc_bias)
        step_size = jax.nn.softplus(columns[moment, :, 2 * STATE:] + dt_bias)
        retain = jnp.exp(step_size * decay_rate)
        ssm_state = retain[:, :, None, None] * ssm_state + (step_size[:, :, None] * x_conv)[:, :, :, None] * bc_conv[:, None, None, :STATE]
        output = jnp.einsum('phen,pn->phe', ssm_state, bc_conv[:, STATE:]) + d_skip[None, :, None] * x_conv
        gated_steps.append(output * jax.nn.silu(projected[0, moment]))
        x_window = x_window[:, 1:]
        bc_window = bc_window[:, 1:]
    gated_all = jnp.stack(gated_steps).reshape(STEPS, -1, HEADS * HEAD_DIM)
    normed_out = rms_scale(gated_all, gate_norm_gain.reshape(-1)).astype(jnp.bfloat16)
    mixed = jnp.dot(normed_out.reshape(-1, HEADS * HEAD_DIM), w_out.reshape(HEADS * HEAD_DIM, D), preferred_element_type=jnp.float32)
    return (mixed.reshape(STEPS, -1, D).astype(jnp.bfloat16), ssm_state)
```

```python
import functools

import jax
import jax.numpy as jnp
from jax import lax
from jax.experimental import pallas as pl
from jax.experimental.pallas import tpu as pltpu
from jax.sharding import PartitionSpec as P

HEADS = 128
HEAD_DIM = 64


epsilon = 1e-05


def entering(shard, axis, combine, identity):
    count, here = (lax.axis_size(axis), lax.axis_index(axis))
    everything = lax.all_gather(shard, axis)
    start = jnp.broadcast_to(jnp.asarray(identity, shard.dtype), shard.shape)

    def step(k, before):
        at = count - 1 - k
        reached = at > here
        new = combine(before, everything[at])
        return jnp.where(reached, new, before)

    return lax.fori_loop(0, count, step, start)


def rms_scale(values, gain):
    return values * lax.rsqrt(jnp.mean(values * values, axis=-1, keepdims=True) + epsilon) * gain


def select_rows(picker, values):
    return jnp.tensordot(picker, values, axes=1, precision=lax.Precision.HIGHEST)


def add_rates(earlier, later_one):
    return earlier + later_one


def per_device(
    token_ids,
    decode_prompt,
    embedding,
    norm_gain,
    w_zx,
    w_bcdt,
    conv_x_weight,
    conv_x_bias,
    conv_bc_weight,
    conv_bc_bias,
    dt_bias,
    a_log,
    d_skip,
    gate_norm_gain,
    w_out,
    state_parts,
    seg_rate,
    x_tail,
    bc_tail,
):
    group = lax.axis_index("dp")
    local_count = state_parts.shape[1]
    slot_count = decode_prompt.shape[0]
    head_count = w_zx.shape[1]
    state_width = conv_bc_bias.shape[0] // 2
    after_rates = entering(seg_rate, "ctx", add_rates, jnp.zeros_like(seg_rate))
    seg_weight = jnp.exp(-after_rates[0])
    scaled = seg_weight[:, :, None, None] * state_parts[0].astype(jnp.float32)
    channel_sums = lax.psum_scatter(
        scaled.astype(jnp.bfloat16), "ctx", scatter_dimension=2, tiled=True
    ).astype(jnp.float32)
    combined = lax.all_to_all(
        channel_sums.astype(jnp.bfloat16), "ctx", split_axis=1, concat_axis=2, tiled=True
    ).astype(channel_sums.dtype)
    tails_x = x_tail.astype(jnp.float32)
    tails_bc = bc_tail.astype(jnp.float32)
    own_slots = lax.dynamic_slice_in_dim(decode_prompt, group * local_count, local_count)
    prompt_ids = jnp.arange(slot_count, dtype=jnp.int32)
    every_state, every_x, every_bc = (
        lax.all_gather(combined.astype(jnp.bfloat16), "dp", axis=0, tiled=True).astype(
            combined.dtype
        ),
        lax.all_gather(tails_x.astype(jnp.bfloat16), "dp", axis=0, tiled=True).astype(
            tails_x.dtype
        ),
        lax.all_gather(tails_bc.astype(jnp.bfloat16), "dp", axis=0, tiled=True).astype(
            tails_bc.dtype
        ),
    )
    picker = (own_slots[:, None] == prompt_ids[None, :]).astype(jnp.float32)
    ssm_state = select_rows(picker, every_state)
    x_window = select_rows(picker, every_x)
    bc_window = select_rows(picker, every_bc)
    vocab_rows = embedding.shape[0]
    holder = (decode_prompt[:, None] == prompt_ids[None, :]).astype(jnp.int32)
    slot_tokens = jnp.sum(token_ids[:, None, :] * holder[None], axis=2)
    offset_tokens = slot_tokens - group * vocab_rows
    inside = (offset_tokens >= 0) & (offset_tokens < vocab_rows)
    looked = jnp.take(embedding, jnp.clip(offset_tokens, 0, vocab_rows - 1), axis=0)
    partial_rows = jnp.where(inside[..., None], looked.astype(jnp.float32), 0.0)
    own_rows = lax.psum_scatter(
        partial_rows.astype(jnp.bfloat16), "dp", scatter_dimension=1, tiled=True
    )
    embedded = lax.all_gather(own_rows, ("ctx", "tp"), axis=2, tiled=True)
    steps_count = embedded.shape[0]
    flat_rows = embedded.reshape(-1, embedded.shape[2]).astype(jnp.float32)
    normed = rms_scale(flat_rows, norm_gain).astype(jnp.bfloat16)
    projected = jnp.einsum("rd,khed->krhe", normed, w_zx, preferred_element_type=jnp.float32)
    projected = projected.reshape(
        2, steps_count, local_count, projected.shape[2], projected.shape[3]
    )
    columns = lax.all_gather(
        jnp.dot(normed, w_bcdt, preferred_element_type=jnp.float32),
        ("ctx", "tp"),
        axis=1,
        tiled=True,
    )
    columns = columns.reshape(steps_count, local_count, -1)
    head_block = lax.axis_index("tp") * lax.axis_size("ctx") + lax.axis_index("ctx")
    head_start = 2 * state_width + head_block * head_count
    dt_raw = lax.dynamic_slice_in_dim(columns, head_start, head_count, 2)
    decay_rate = -jnp.exp(a_log)
    gated_steps = []
    for moment in range(steps_count):
        x_window = jnp.concatenate([x_window, projected[1, moment][:, None]], axis=1)
        bc_window = jnp.concatenate(
            [bc_window, columns[moment, :, None, : 2 * state_width]], axis=1
        )
        x_conv = jax.nn.silu(jnp.einsum("pkhe,khe->phe", x_window, conv_x_weight) + conv_x_bias)
        bc_conv = jax.nn.silu(jnp.einsum("pkn,kn->pn", bc_window, conv_bc_weight) + conv_bc_bias)
        step_size = jax.nn.softplus(dt_raw[moment] + dt_bias)
        retain = jnp.exp(step_size * decay_rate)
        ssm_state = (
            retain[:, :, None, None] * ssm_state
            + (step_size[:, :, None] * x_conv)[:, :, :, None] * bc_conv[:, None, None, :state_width]
        )
        output = (
            jnp.einsum("phen,pn->phe", ssm_state, bc_conv[:, state_width:])
            + d_skip[None, :, None] * x_conv
        )
        gated_steps.append(output * jax.nn.silu(projected[0, moment]))
        x_window = x_window[:, 1:]
        bc_window = bc_window[:, 1:]
    gated_all = jnp.stack(gated_steps)
    local_squares = jnp.sum(gated_all * gated_all, axis=(2, 3))
    total_squares = lax.psum(local_squares, ("ctx", "tp"))
    inverse = lax.rsqrt(total_squares / (HEADS * HEAD_DIM) + epsilon)
    normed_out = (gated_all * inverse[:, :, None, None] * gate_norm_gain).astype(jnp.bfloat16)
    partial_out = jnp.einsum("tphe,hed->tpd", normed_out, w_out, preferred_element_type=jnp.float32)
    outer_sum = lax.psum_scatter(
        partial_out.astype(jnp.bfloat16), "ctx", scatter_dimension=2, tiled=True
    ).astype(jnp.float32)
    mixed = lax.psum_scatter(outer_sum, "tp", scatter_dimension=2, tiled=True)
    return (mixed.astype(jnp.bfloat16), ssm_state)


HI = lax.Precision.HIGHEST
F32 = jnp.float32
BF16 = jnp.bfloat16


def f32_dot(a, b):
    return jnp.dot(a, b, precision=HI, preferred_element_type=F32)


def nt_dot(a, b):
    return lax.dot_general(a, b, (((1,), (1,)), ((), ())), preferred_element_type=F32)


def silu(v):
    return v / (1.0 + jnp.exp(-v))


def softplus(v):
    return jnp.maximum(v, 0.0) + jnp.log1p(jnp.exp(-jnp.abs(v)))


ROW_TILE = 16


def gather_kernel(steps, slots, groups, tok_ref, dec_ref, emb_ref, out_ref, buf, tail, sems, tail_sem):
    vocab = emb_ref.shape[0]
    whole = vocab // ROW_TILE * ROW_TILE
    base = lax.axis_index("dp") * vocab
    per_group = slots // groups
    tail_copy = None
    if whole < vocab:
        tail_copy = pltpu.make_async_copy(emb_ref.at[pl.ds(whole, vocab - whole)], tail, tail_sem)
        tail_copy.start()
    copies = []
    where = []
    for s in range(slots):
        q = dec_ref[s]
        for t in range(steps):
            row = tok_ref[t, q] - base
            clipped = jnp.clip(row, 0, vocab - 1)
            start = jnp.minimum(clipped // ROW_TILE * ROW_TILE, whole - ROW_TILE)
            start = pl.multiple_of(start, ROW_TILE)
            i = s * steps + t
            copy = pltpu.make_async_copy(emb_ref.at[pl.ds(start, ROW_TILE)], buf.at[i], sems.at[i])
            copy.start()
            copies.append(copy)
            where.append((row, start))
    if tail_copy is not None:
        tail_copy.wait()
    for copy in copies:
        copy.wait()
    rows = lax.broadcasted_iota(jnp.int32, (ROW_TILE, 1), 0)
    for g in range(groups):
        picked = []
        for t in range(steps):
            for j in range(per_group):
                i = (g * per_group + j) * steps + t
                row, start = where[i]
                value = jnp.sum(
                    jnp.where(rows == row - start, buf[i].astype(F32), 0.0), axis=0, keepdims=True
                )
                if tail_copy is not None:
                    trows = lax.broadcasted_iota(jnp.int32, (vocab - whole, 1), 0)
                    value += jnp.sum(
                        jnp.where(trows == row - whole, tail[...].astype(F32), 0.0),
                        axis=0,
                        keepdims=True,
                    )
                picked.append(value)
        out_ref[g] = jnp.concatenate(picked, axis=0).astype(BF16)


def mixer_kernel(
    sizes,
    dec_ref,
    part_ref,
    gain_ref,
    cxw_ref,
    cxb_ref,
    cbw_ref,
    cbb_ref,
    dtb_ref,
    alog_ref,
    skip_ref,
    gg_ref,
    seg_ref,
    xt_ref,
    bt_ref,
    wzx_hbm,
    wbc_hbm,
    wout_hbm,
    state_hbm,
    mixed_ref,
    final_ref,
    wzx,
    wbc,
    wout,
    state_in,
    state_send,
    state_recv,
    emb_recv,
    seg_recv,
    xt_recv,
    bt_recv,
    col_send,
    col_recv,
    sq_send,
    sq_recv,
    out_send,
    out_recv,
    start_state,
    xfull,
    bcfull,
    gated_ref,
    load_sems,
    own_sem,
    emb_sems,
    state_sems,
    seg_sems,
    xt_sems,
    bt_sems,
    col_sems,
    sq_sems,
    out_sems,
):
    n_ctx, n_dp, n_tp, total_heads = sizes
    c, d, p = lax.axis_index("ctx"), lax.axis_index("dp"), lax.axis_index("tp")
    mine = c * n_tp + p
    steps, per, feats = mixed_ref.shape
    rows = steps * per
    heads, dim = cxb_ref.shape
    chans = heads * dim
    width = cbb_ref.shape[1]
    state_n = width // 2
    taps = cxw_ref.shape[0]
    model = gain_ref.shape[1]
    tp_heads = seg_ref.shape[-1]
    n_cols = wbc_hbm.shape[1]
    all_cols = n_cols * n_ctx * n_tp

    loads = []
    half = wzx_hbm.shape[0] // 2
    pairs = (
        (state_hbm, state_in),
        (wbc_hbm, wbc),
        (wzx_hbm.at[pl.ds(half, half)], wzx.at[pl.ds(half, half)]),
        (wzx_hbm.at[pl.ds(0, half)], wzx.at[pl.ds(0, half)]),
        (wout_hbm, wout),
    )
    for i, (source, target) in enumerate(pairs):
        load = pltpu.make_async_copy(source, target, load_sems.at[i])
        load.start()
        loads.append(load)

    def peer(offset):
        dc, dd, dt = offset
        return lax.rem(c + dc, n_ctx), lax.rem(d + dd, n_dp), lax.rem(p + dt, n_tp)

    def device(offset):
        a, b, e = peer(offset)
        return {"ctx": a, "dp": b, "tp": e}

    everyone = [
        (a, b, e) for a in range(n_ctx) for b in range(n_dp) for e in range(n_tp) if a + b + e
    ]
    everyone.sort(key=lambda o: -(min(o[2], n_tp - o[2]) * 4 + o[1] * 2 + o[0]))
    group = [o for o in everyone if o[1] == 0]
    routed = [o for o in everyone if o[2] == 0]
    across = [o for o in everyone if o[0] == 0 and o[2] == 0]

    barrier = pltpu.get_barrier_semaphore()
    for o in everyone:
        pl.semaphore_signal(
            barrier, inc=1, device_id=device(o), device_id_type=pl.DeviceIdType.MESH
        )

    def send(source, target, sems, slot, offset):
        copy = pltpu.make_async_remote_copy(
            src_ref=source,
            dst_ref=target,
            send_sem=sems.at[0, slot],
            recv_sem=sems.at[1, slot],
            device_id=device(offset),
            device_id_type=pl.DeviceIdType.MESH,
        )
        copy.start()
        return copy

    loads[0].wait()
    for g in range(n_dp):
        pick = jnp.int32(0)
        for j in range(per):
            local = dec_ref[g * per + j] - d * per
            pick += jnp.where((local >= 0) & (local < per), local, 0)
        state_send[g] = state_in[pick]

    col_send[...] = jnp.zeros_like(col_send)

    pl.semaphore_wait(barrier, len(everyone))

    emb_copies = [
        send(part_ref.at[peer(o)[1]], emb_recv.at[d, mine], emb_sems, i, o)
        for i, o in enumerate(everyone)
    ]
    emb_recv[d, mine] = part_ref[d]
    seg_copies = [send(seg_ref.at[0], seg_recv.at[d, c], seg_sems, i, o) for i, o in enumerate(routed)]
    xt_copies = [send(xt_ref, xt_recv.at[d], xt_sems, i, o) for i, o in enumerate(across)]
    bt_copies = [send(bt_ref, bt_recv.at[d], bt_sems, i, o) for i, o in enumerate(across)]
    state_copies = []
    for i, o in enumerate(routed):
        pc, pd, _ = peer(o)
        source = state_send.at[pd, pl.ds(pl.multiple_of(pc * chans, chans), chans)]
        state_copies.append(send(source, state_recv.at[d, c], state_sems, i, o))
    own = pltpu.make_async_copy(
        state_send.at[d, pl.ds(pl.multiple_of(c * chans, chans), chans)],
        state_recv.at[d, c],
        own_sem,
    )
    own.start()
    seg_recv[d, c] = seg_ref[0]
    xt_recv[d] = xt_ref[...]
    bt_recv[d] = bt_ref[...]

    lane = lax.broadcasted_iota(jnp.int32, (1, chans), 1)
    fold = (
        lax.broadcasted_iota(jnp.int32, (dim, chans), 0)
        == lax.rem(lax.broadcasted_iota(jnp.int32, (dim, chans), 1), dim)
    ).astype(F32)
    head_rows = lax.broadcasted_iota(jnp.int32, (heads, chans), 0) == lax.div(
        lax.broadcasted_iota(jnp.int32, (heads, chans), 1), dim
    )

    def flat(value):
        return jnp.sum(jnp.where(head_rows, f32_dot(value, fold), 0.0), axis=0, keepdims=True)

    def spread(value, first):
        count = value.shape[1]
        chosen = (
            lax.broadcasted_iota(jnp.int32, (count, chans), 0)
            == first + lax.div(lax.broadcasted_iota(jnp.int32, (count, chans), 1), dim)
        ).astype(F32)
        return f32_dot(value, chosen)

    tap_rows = [flat(cxw_ref[k]) for k in range(taps)]
    bias_row = flat(cxb_ref[...])
    gate_row = flat(gg_ref[...])
    dtb_row = spread(dtb_ref[...], 0)
    rate_row = -jnp.exp(spread(alog_ref[...], 0))
    skip_row = spread(skip_ref[...], 0)

    for copy in emb_copies:
        copy.wait_recv()
    pieces = []
    for i in range(n_ctx * n_tp):
        piece = emb_recv[0, i].astype(F32)
        for g in range(1, n_dp):
            piece += emb_recv[g, i].astype(F32)
        pieces.append(piece)
    embedded = jnp.concatenate(pieces, axis=1)
    scale = lax.rsqrt(jnp.sum(embedded * embedded, axis=1, keepdims=True) / model + epsilon)
    normed = (embedded * scale * gain_ref[...]).astype(BF16)
    loads[1].wait()
    col_send[:, 0:n_cols] = jnp.dot(normed, wbc[...], preferred_element_type=F32)
    col_copies = [send(col_send, col_recv.at[mine], col_sems, i, o) for i, o in enumerate(group)]
    col_recv[mine] = col_send[...]
    loads[2].wait()
    x_rows = nt_dot(normed, wzx[half : 2 * half, :])
    loads[3].wait()
    z_gate = silu(nt_dot(normed, wzx[0:half, :]))

    for copy in xt_copies + bt_copies:
        copy.wait_recv()
    holders = [lax.div(dec_ref[d * per + j], per) for j in range(per)]
    places = [lax.rem(dec_ref[d * per + j], per) for j in range(per)]
    for k in range(taps - 1):
        for j in range(per):
            r = k * per + j
            xfull[r : r + 1, :] = flat(xt_recv[holders[j], places[j], k].astype(F32))
            bcfull[r : r + 1, :] = bt_recv[holders[j], places[j], pl.ds(k, 1), :].astype(F32)
    lead = (taps - 1) * per
    xfull[lead : lead + rows, :] = x_rows
    conv = bias_row
    for k in range(taps):
        conv = conv + tap_rows[k] * xfull[k * per : k * per + rows, :]
    xc = silu(conv)

    for copy in seg_copies:
        copy.wait_recv()
    weights = []
    for j in range(per):
        after = jnp.zeros((1, tp_heads), F32)
        ordered = []
        for k in reversed(range(n_ctx)):
            ordered.append(jnp.exp(-after))
            after = after + seg_recv[holders[j], k, pl.ds(places[j], 1), :]
        weights.extend(reversed(ordered))
    weight_cols = jnp.transpose(spread(jnp.concatenate(weights, axis=0), c * heads))
    own.wait()
    for copy in state_copies:
        copy.wait_recv()
    for j in range(per):
        total = None
        for k in range(n_ctx):
            r = j * n_ctx + k
            term = weight_cols[:, r : r + 1] * state_recv[holders[j], k].astype(F32)
            total = term if total is None else total + term
        start_state[j] = total

    for copy in col_copies:
        copy.wait_recv()
    wide_pad = jnp.zeros((rows, all_cols - col_send.shape[1]), F32)
    columns = jnp.zeros((rows, all_cols), F32)
    for i in range(n_ctx * n_tp):
        wide = jnp.concatenate([col_recv[i], wide_pad], axis=1)
        columns = columns + (pltpu.roll(wide, n_cols * i, 1) if i else wide)
    bcfull[lead : lead + rows, :] = columns[:, :width]
    conv = cbb_ref[...]
    for k in range(taps):
        conv = conv + cbw_ref[k : k + 1, :] * bcfull[k * per : k * per + rows, :]
    bcc = silu(conv)
    b_all, c_all = bcc[:, :state_n], bcc[:, state_n:]
    head_first = (p * n_ctx + c) * heads
    step_size = softplus(spread(columns[:, width:], head_first) + dtb_row)
    log_keep = step_size * rate_row
    driven = step_size * xc

    row_slot = lax.rem(lax.broadcasted_iota(jnp.int32, (rows, 1), 0), per)
    from_start = jnp.zeros((rows, chans), F32)
    c_low = c_all.astype(BF16)
    for j in range(per):
        from_start += jnp.where(row_slot == j, nt_dot(c_low, start_state[j].astype(BF16)), 0.0)

    def at(value, t):
        return value[t * per : (t + 1) * per]

    total = jnp.zeros((per, chans), F32)
    sums = []
    for t in range(steps):
        total = total + at(log_keep, t)
        sums.append(total)
    for t in range(steps):
        y = jnp.exp(sums[t]) * at(from_start, t) + skip_row * at(xc, t)
        for s in range(t + 1):
            overlap = jnp.sum(at(b_all, s) * at(c_all, t), axis=1, keepdims=True)
            term = at(driven, s) * overlap
            y = y + (term if s == t else jnp.exp(sums[t] - sums[s]) * term)
        gated_ref[t * per : (t + 1) * per, :] = y
    gated = gated_ref[...] * z_gate
    squares = jnp.sum(gated * gated, axis=1, keepdims=True)
    sq_send[...] = jnp.broadcast_to(squares, sq_send.shape)
    sq_copies = [send(sq_send, sq_recv.at[mine], sq_sems, i, o) for i, o in enumerate(group)]
    sq_recv[mine] = sq_send[...]

    loads[4].wait()
    partial = jnp.dot((gated * gate_row).astype(BF16), wout[...], preferred_element_type=F32)
    for i in range(n_ctx * n_tp):
        out_send[i] = partial[:, i * feats : (i + 1) * feats].astype(BF16)
    out_copies = []
    for i, o in enumerate(group):
        pc, _, pp = peer(o)
        out_copies.append(send(out_send.at[pc * n_tp + pp], out_recv.at[mine], out_sems, i, o))
    out_recv[mine] = out_send[mine]

    late = [jnp.exp(sums[-1] - sums[t]) * at(driven, t) for t in range(steps)]
    flat_rows = jnp.concatenate(late + [jnp.exp(sums[-1])] * (rows // per), axis=0)
    tall = jnp.transpose(flat_rows)
    for j in range(per):
        b_own = jnp.where(row_slot == j, b_all, 0.0)
        final_ref[j] = (
            tall[:, rows + j : rows + j + 1] * start_state[j] + f32_dot(tall[:, :rows], b_own)
        )

    for copy in sq_copies + out_copies:
        copy.wait_recv()
    total_squares = sq_recv[0]
    mixed = out_recv[0].astype(F32)
    for i in range(1, n_ctx * n_tp):
        total_squares = total_squares + sq_recv[i]
        mixed = mixed + out_recv[i].astype(F32)
    inverse = lax.rsqrt(total_squares[:, 0:1] / (total_heads * dim) + epsilon)
    mixed = mixed * inverse
    for t in range(steps):
        mixed_ref[t] = at(mixed, t).astype(BF16)
    for copy in (
        emb_copies + seg_copies + xt_copies + bt_copies + state_copies + col_copies + sq_copies
        + out_copies
    ):
        copy.wait_send()


def kernel_device(
    sizes,
    token_ids,
    decode_prompt,
    embedding,
    norm_gain,
    w_zx,
    w_bcdt,
    conv_x_weight,
    conv_x_bias,
    conv_bc_weight,
    conv_bc_bias,
    dt_bias,
    a_log,
    d_skip,
    gate_norm_gain,
    w_out,
    state_parts,
    seg_rate,
    x_tail,
    bc_tail,
):
    n_ctx, n_dp, n_tp, _ = sizes
    steps = token_ids.shape[0]
    slots = decode_prompt.shape[0]
    per = state_parts.shape[1]
    rows = steps * per
    vocab, feats = embedding.shape
    heads, dim, model = w_zx.shape[1:]
    chans = heads * dim
    tp_heads, state_n = state_parts.shape[2], state_parts.shape[4]
    world, ring = n_ctx * n_dp * n_tp, n_ctx * n_tp
    smem = pl.BlockSpec(memory_space=pltpu.SMEM)
    vmem = pl.BlockSpec(memory_space=pltpu.VMEM)
    anywhere = pl.BlockSpec(memory_space=pl.ANY)
    rest = max(1, vocab % ROW_TILE)
    part = pl.pallas_call(
        functools.partial(gather_kernel, steps, slots, n_dp),
        out_shape=jax.ShapeDtypeStruct((n_dp, rows, feats), BF16),
        in_specs=[smem, smem, anywhere],
        out_specs=vmem,
        scratch_shapes=[
            pltpu.VMEM((steps * slots, ROW_TILE, feats), BF16),
            pltpu.VMEM((rest, feats), BF16),
            pltpu.SemaphoreType.DMA((steps * slots,)),
            pltpu.SemaphoreType.DMA,
        ],
        name="gather_rows",
    )(token_ids, decode_prompt, embedding)
    sem = pltpu.SemaphoreType.DMA
    wide = 2 * state_n
    full_rows = -(-(conv_x_weight.shape[0] - 1 + steps) * per // 8) * 8
    mixed, final = pl.pallas_call(
        functools.partial(mixer_kernel, sizes),
        out_shape=(
            jax.ShapeDtypeStruct((steps, per, feats), BF16),
            jax.ShapeDtypeStruct((per, chans, state_n), F32),
        ),
        in_specs=[smem] + [vmem] * 13 + [anywhere] * 4,
        out_specs=(vmem, vmem),
        scratch_shapes=[
            pltpu.VMEM((2 * chans, model), BF16),
            pltpu.VMEM(w_bcdt.shape, BF16),
            pltpu.VMEM((chans, model), BF16),
            pltpu.VMEM((per, tp_heads * dim, state_n), BF16),
            pltpu.VMEM((n_dp, tp_heads * dim, state_n), BF16),
            pltpu.VMEM((n_dp, n_ctx, chans, state_n), BF16),
            pltpu.VMEM((n_dp, ring, rows, feats), BF16),
            pltpu.VMEM((n_dp, n_ctx, per, tp_heads), F32),
            pltpu.VMEM((n_dp,) + x_tail.shape, BF16),
            pltpu.VMEM((n_dp,) + bc_tail.shape, BF16),
            pltpu.VMEM((rows, 128), F32),
            pltpu.VMEM((ring, rows, 128), F32),
            pltpu.VMEM((rows, 128), F32),
            pltpu.VMEM((ring, rows, 128), F32),
            pltpu.VMEM((ring, rows, feats), BF16),
            pltpu.VMEM((ring, rows, feats), BF16),
            pltpu.VMEM((per, chans, state_n), F32),
            pltpu.VMEM((full_rows, chans), F32),
            pltpu.VMEM((full_rows, wide), F32),
            pltpu.VMEM((rows, chans), F32),
            sem((5,)),
            sem,
            sem((2, world)),
            sem((2, n_ctx * n_dp)),
            sem((2, n_ctx * n_dp)),
            sem((2, n_dp)),
            sem((2, n_dp)),
            sem((2, ring)),
            sem((2, ring)),
            sem((2, ring)),
        ],
        compiler_params=pltpu.CompilerParams(
            collective_id=0, has_side_effects=True, vmem_limit_bytes=56 * 1024 * 1024
        ),
        name="mixer",
    )(
        decode_prompt,
        part,
        norm_gain[None],
        conv_x_weight,
        conv_x_bias,
        conv_bc_weight,
        conv_bc_bias[None],
        dt_bias[None],
        a_log[None],
        d_skip[None],
        gate_norm_gain,
        seg_rate,
        x_tail,
        bc_tail,
        w_zx.reshape(2 * chans, model),
        w_bcdt,
        w_out.reshape(chans, model),
        state_parts.reshape(per, tp_heads * dim, state_n),
    )
    return mixed, final.reshape(per, heads, dim, state_n)


def choose_device(sizes, *args):
    embedding, w_zx, w_bcdt = args[2], args[4], args[5]
    heads, dim = w_zx.shape[1:3]
    fits = (
        embedding.shape[1] % 128 == 0
        and (heads * dim) % 128 == 0
        and w_bcdt.shape[1] <= 128
        and embedding.shape[0] >= ROW_TILE
    )
    if fits:
        return kernel_device(sizes, *args)
    return per_device(*args)


def solution(mesh):
    sizes = (mesh.shape["ctx"], mesh.shape["dp"], mesh.shape["tp"], HEADS)
    return jax.shard_map(
        functools.partial(choose_device, sizes),
        mesh=mesh,
        in_specs=(
            P(),
            P(),
            P("dp", ("ctx", "tp")),
            P(),
            P(None, ("tp", "ctx"), None, None),
            P(None, ("ctx", "tp")),
            P(None, ("tp", "ctx"), None),
            P(("tp", "ctx"), None),
            P(),
            P(),
            P(("tp", "ctx")),
            P(("tp", "ctx")),
            P(("tp", "ctx")),
            P(("tp", "ctx"), None),
            P(("tp", "ctx"), None, None),
            P("ctx", "dp", "tp", None, None),
            P("ctx", "dp", "tp"),
            P("dp", None, ("tp", "ctx"), None),
            P("dp", None, None),
        ),
        out_specs=(P(None, "dp", ("ctx", "tp")), P("dp", ("tp", "ctx"), None, None)),
        check_vma=False,
    )
```

```python
import functools

import jax
import jax.numpy as jnp
from jax import lax
from jax.experimental import pallas as pl
from jax.experimental.pallas import tpu as pltpu
from jax.sharding import PartitionSpec as P

HEADS = 128
HEAD_DIM = 64


epsilon = 1e-05


def entering(shard, axis, combine, identity):
    count, here = (lax.axis_size(axis), lax.axis_index(axis))
    everything = lax.all_gather(shard, axis)
    start = jnp.broadcast_to(jnp.asarray(identity, shard.dtype), shard.shape)

    def step(k, before):
        at = count - 1 - k
        reached = at > here
        new = combine(before, everything[at])
        return jnp.where(reached, new, before)

    return lax.fori_loop(0, count, step, start)


def rms_scale(values, gain):
    return values * lax.rsqrt(jnp.mean(values * values, axis=-1, keepdims=True) + epsilon) * gain


def select_rows(picker, values):
    return jnp.tensordot(picker, values, axes=1, precision=lax.Precision.HIGHEST)


def add_rates(earlier, later_one):
    return earlier + later_one


def per_device(
    token_ids,
    decode_prompt,
    embedding,
    norm_gain,
    w_zx,
    w_bcdt,
    conv_x_weight,
    conv_x_bias,
    conv_bc_weight,
    conv_bc_bias,
    dt_bias,
    a_log,
    d_skip,
    gate_norm_gain,
    w_out,
    state_parts,
    seg_rate,
    x_tail,
    bc_tail,
):
    group = lax.axis_index("dp")
    local_count = state_parts.shape[1]
    slot_count = decode_prompt.shape[0]
    head_count = w_zx.shape[1]
    state_width = conv_bc_bias.shape[0] // 2
    after_rates = entering(seg_rate, "ctx", add_rates, jnp.zeros_like(seg_rate))
    seg_weight = jnp.exp(-after_rates[0])
    scaled = seg_weight[:, :, None, None] * state_parts[0].astype(jnp.float32)
    channel_sums = lax.psum_scatter(
        scaled.astype(jnp.bfloat16), "ctx", scatter_dimension=2, tiled=True
    ).astype(jnp.float32)
    combined = lax.all_to_all(
        channel_sums.astype(jnp.bfloat16), "ctx", split_axis=1, concat_axis=2, tiled=True
    ).astype(channel_sums.dtype)
    tails_x = x_tail.astype(jnp.float32)
    tails_bc = bc_tail.astype(jnp.float32)
    own_slots = lax.dynamic_slice_in_dim(decode_prompt, group * local_count, local_count)
    prompt_ids = jnp.arange(slot_count, dtype=jnp.int32)
    every_state, every_x, every_bc = (
        lax.all_gather(combined.astype(jnp.bfloat16), "dp", axis=0, tiled=True).astype(
            combined.dtype
        ),
        lax.all_gather(tails_x.astype(jnp.bfloat16), "dp", axis=0, tiled=True).astype(
            tails_x.dtype
        ),
        lax.all_gather(tails_bc.astype(jnp.bfloat16), "dp", axis=0, tiled=True).astype(
            tails_bc.dtype
        ),
    )
    picker = (own_slots[:, None] == prompt_ids[None, :]).astype(jnp.float32)
    ssm_state = select_rows(picker, every_state)
    x_window = select_rows(picker, every_x)
    bc_window = select_rows(picker, every_bc)
    vocab_rows = embedding.shape[0]
    holder = (decode_prompt[:, None] == prompt_ids[None, :]).astype(jnp.int32)
    slot_tokens = jnp.sum(token_ids[:, None, :] * holder[None], axis=2)
    offset_tokens = slot_tokens - group * vocab_rows
    inside = (offset_tokens >= 0) & (offset_tokens < vocab_rows)
    looked = jnp.take(embedding, jnp.clip(offset_tokens, 0, vocab_rows - 1), axis=0)
    partial_rows = jnp.where(inside[..., None], looked.astype(jnp.float32), 0.0)
    own_rows = lax.psum_scatter(
        partial_rows.astype(jnp.bfloat16), "dp", scatter_dimension=1, tiled=True
    )
    embedded = lax.all_gather(own_rows, ("ctx", "tp"), axis=2, tiled=True)
    steps_count = embedded.shape[0]
    flat_rows = embedded.reshape(-1, embedded.shape[2]).astype(jnp.float32)
    normed = rms_scale(flat_rows, norm_gain).astype(jnp.bfloat16)
    projected = jnp.einsum("rd,khed->krhe", normed, w_zx, preferred_element_type=jnp.float32)
    projected = projected.reshape(
        2, steps_count, local_count, projected.shape[2], projected.shape[3]
    )
    columns = lax.all_gather(
        jnp.dot(normed, w_bcdt, preferred_element_type=jnp.float32),
        ("ctx", "tp"),
        axis=1,
        tiled=True,
    )
    columns = columns.reshape(steps_count, local_count, -1)
    head_block = lax.axis_index("tp") * lax.axis_size("ctx") + lax.axis_index("ctx")
    head_start = 2 * state_width + head_block * head_count
    dt_raw = lax.dynamic_slice_in_dim(columns, head_start, head_count, 2)
    decay_rate = -jnp.exp(a_log)
    gated_steps = []
    for moment in range(steps_count):
        x_window = jnp.concatenate([x_window, projected[1, moment][:, None]], axis=1)
        bc_window = jnp.concatenate(
            [bc_window, columns[moment, :, None, : 2 * state_width]], axis=1
        )
        x_conv = jax.nn.silu(jnp.einsum("pkhe,khe->phe", x_window, conv_x_weight) + conv_x_bias)
        bc_conv = jax.nn.silu(jnp.einsum("pkn,kn->pn", bc_window, conv_bc_weight) + conv_bc_bias)
        step_size = jax.nn.softplus(dt_raw[moment] + dt_bias)
        retain = jnp.exp(step_size * decay_rate)
        ssm_state = (
            retain[:, :, None, None] * ssm_state
            + (step_size[:, :, None] * x_conv)[:, :, :, None] * bc_conv[:, None, None, :state_width]
        )
        output = (
            jnp.einsum("phen,pn->phe", ssm_state, bc_conv[:, state_width:])
            + d_skip[None, :, None] * x_conv
        )
        gated_steps.append(output * jax.nn.silu(projected[0, moment]))
        x_window = x_window[:, 1:]
        bc_window = bc_window[:, 1:]
    gated_all = jnp.stack(gated_steps)
    local_squares = jnp.sum(gated_all * gated_all, axis=(2, 3))
    total_squares = lax.psum(local_squares, ("ctx", "tp"))
    inverse = lax.rsqrt(total_squares / (HEADS * HEAD_DIM) + epsilon)
    normed_out = (gated_all * inverse[:, :, None, None] * gate_norm_gain).astype(jnp.bfloat16)
    partial_out = jnp.einsum("tphe,hed->tpd", normed_out, w_out, preferred_element_type=jnp.float32)
    outer_sum = lax.psum_scatter(
        partial_out.astype(jnp.bfloat16), "ctx", scatter_dimension=2, tiled=True
    ).astype(jnp.float32)
    mixed = lax.psum_scatter(outer_sum, "tp", scatter_dimension=2, tiled=True)
    return (mixed.astype(jnp.bfloat16), ssm_state)


HI = lax.Precision.HIGHEST
F32 = jnp.float32
BF16 = jnp.bfloat16


def f32_dot(a, b):
    return jnp.dot(a, b, precision=HI, preferred_element_type=F32)


def nt_dot(a, b):
    return lax.dot_general(a, b, (((1,), (1,)), ((), ())), preferred_element_type=F32)


def silu(v):
    return v / (1.0 + jnp.exp(-v))


def softplus(v):
    return jnp.maximum(v, 0.0) + jnp.log1p(jnp.exp(-jnp.abs(v)))


ROW_TILE = 16


def gather_kernel(steps, slots, groups, tok_ref, dec_ref, emb_ref, out_ref, buf, tail, sems, tail_sem):
    vocab = emb_ref.shape[0]
    whole = vocab // ROW_TILE * ROW_TILE
    base = lax.axis_index("dp") * vocab
    per_group = slots // groups
    tail_copy = None
    if whole < vocab:
        tail_copy = pltpu.make_async_copy(emb_ref.at[pl.ds(whole, vocab - whole)], tail, tail_sem)
        tail_copy.start()
    copies = []
    where = []
    for s in range(slots):
        q = dec_ref[s]
        for t in range(steps):
            row = tok_ref[t, q] - base
            clipped = jnp.clip(row, 0, vocab - 1)
            start = jnp.minimum(clipped // ROW_TILE * ROW_TILE, whole - ROW_TILE)
            start = pl.multiple_of(start, ROW_TILE)
            i = s * steps + t
            copy = pltpu.make_async_copy(emb_ref.at[pl.ds(start, ROW_TILE)], buf.at[i], sems.at[i])
            copy.start()
            copies.append(copy)
            where.append((row, start))
    if tail_copy is not None:
        tail_copy.wait()
    for copy in copies:
        copy.wait()
    rows = lax.broadcasted_iota(jnp.int32, (ROW_TILE, 1), 0)
    for g in range(groups):
        picked = []
        for t in range(steps):
            for j in range(per_group):
                i = (g * per_group + j) * steps + t
                row, start = where[i]
                value = jnp.sum(
                    jnp.where(rows == row - start, buf[i].astype(F32), 0.0), axis=0, keepdims=True
                )
                if tail_copy is not None:
                    trows = lax.broadcasted_iota(jnp.int32, (vocab - whole, 1), 0)
                    value += jnp.sum(
                        jnp.where(trows == row - whole, tail[...].astype(F32), 0.0),
                        axis=0,
                        keepdims=True,
                    )
                picked.append(value)
        out_ref[g] = jnp.concatenate(picked, axis=0).astype(BF16)


def mixer_kernel(
    sizes,
    dec_ref,
    part_ref,
    seg_ref,
    xt_ref,
    bt_ref,
    gain_hbm,
    cxw_hbm,
    cxb_hbm,
    cbw_hbm,
    cbb_hbm,
    dtb_hbm,
    alog_hbm,
    skip_hbm,
    gg_hbm,
    wzx_hbm,
    wbc_hbm,
    wout_hbm,
    state_hbm,
    mixed_ref,
    final_hbm,
    gain_ref,
    cxw_ref,
    cxb_ref,
    cbw_ref,
    cbb_ref,
    dtb_ref,
    alog_ref,
    skip_ref,
    gg_ref,
    final_ref,
    pair_recv,
    pair_send,
    wzx,
    wbc,
    wout,
    state_in,
    state_send,
    state_recv,
    emb_recv,
    seg_recv,
    xt_recv,
    bt_recv,
    col_send,
    col_recv,
    sq_send,
    sq_recv,
    out_send,
    out_recv,
    start_state,
    xfull,
    bcfull,
    gated_ref,
    load_sems,
    small_sems,
    own_sems,
    final_sem,
    pair_sems,
    emb_sems,
    state_sems,
    seg_sems,
    xt_sems,
    bt_sems,
    col_sems,
    sq_sems,
    out_sems,
):
    n_ctx, n_dp, n_tp, total_heads = sizes
    c, d, p = lax.axis_index("ctx"), lax.axis_index("dp"), lax.axis_index("tp")
    mine = c * n_tp + p
    steps, per, feats = mixed_ref.shape
    rows = steps * per
    heads, dim = cxb_ref.shape
    chans = heads * dim
    width = cbb_ref.shape[1]
    state_n = width // 2
    taps = cxw_ref.shape[0]
    model = gain_ref.shape[1]
    tp_heads = seg_ref.shape[-1]
    n_cols = wbc_hbm.shape[0]
    all_cols = n_cols * n_ctx * n_tp

    def peer(offset):
        dc, dd, dt = offset
        return lax.rem(c + dc, n_ctx), lax.rem(d + dd, n_dp), lax.rem(p + dt, n_tp)

    def device(offset):
        a, b, e = peer(offset)
        return {"ctx": a, "dp": b, "tp": e}

    everyone = [
        (a, b, e) for a in range(n_ctx) for b in range(n_dp) for e in range(n_tp) if a + b + e
    ]
    everyone.sort(key=lambda o: -(min(o[2], n_tp - o[2]) * 4 + o[1] * 2 + o[0]))
    group = [o for o in everyone if o[1] == 0]
    beside = [o for o in group if o[2] == 0]
    across = [o for o in everyone if o[0] == 0 and o[2] == 0]

    barrier = pltpu.get_barrier_semaphore()
    for o in everyone:
        pl.semaphore_signal(
            barrier, inc=1, device_id=device(o), device_id_type=pl.DeviceIdType.MESH
        )

    loads = []
    half = wzx_hbm.shape[0] // 2
    pairs = (
        (state_hbm, state_in),
        (wbc_hbm, wbc),
        (wzx_hbm.at[pl.ds(half, half)], wzx.at[pl.ds(half, half)]),
        (wzx_hbm.at[pl.ds(0, half)], wzx.at[pl.ds(0, half)]),
        (wout_hbm, wout),
    )
    for i, (source, target) in enumerate(pairs):
        load = pltpu.make_async_copy(source, target, load_sems.at[i])
        load.start()
        loads.append(load)

    small_pairs = (
        (gain_hbm, gain_ref),
        (cxw_hbm, cxw_ref),
        (cxb_hbm, cxb_ref),
        (cbw_hbm, cbw_ref),
        (cbb_hbm, cbb_ref),
        (dtb_hbm, dtb_ref),
        (alog_hbm, alog_ref),
        (skip_hbm, skip_ref),
        (gg_hbm, gg_ref),
    )
    smalls = []
    for i, (source, target) in enumerate(small_pairs):
        load = pltpu.make_async_copy(source, target, small_sems.at[i])
        load.start()
        smalls.append(load)
    owns = []
    for source, target in (
        (part_ref.at[d], emb_recv.at[d, mine]),
        (seg_ref.at[0], seg_recv.at[c]),
        (xt_ref, xt_recv.at[d]),
        (bt_ref, bt_recv.at[d]),
    ):
        load = pltpu.make_async_copy(source, target, own_sems.at[len(owns)])
        load.start()
        owns.append(load)

    def send(source, target, sems, slot, offset):
        copy = pltpu.make_async_remote_copy(
            src_ref=source,
            dst_ref=target,
            send_sem=sems.at[0, slot],
            recv_sem=sems.at[1, slot],
            device_id=device(offset),
            device_id_type=pl.DeviceIdType.MESH,
        )
        copy.start()
        return copy

    loads[0].wait()
    picks = []
    for g in range(n_dp):
        pick = jnp.int32(0)
        for j in range(per):
            local = dec_ref[g * per + j] - d * per
            pick += jnp.where((local >= 0) & (local < per), local, 0)
        state_send[g] = state_in[pick]
        picks.append(pick)

    col_send[...] = jnp.zeros_like(col_send)

    pl.semaphore_wait(barrier, len(everyone))

    emb_copies = [
        send(part_ref.at[peer(o)[1]], emb_recv.at[d, mine], emb_sems, i, o)
        for i, o in enumerate(everyone)
    ]
    seg_copies = [send(seg_ref.at[0], seg_recv.at[c], seg_sems, i, o) for i, o in enumerate(beside)]
    parity = lax.rem(c, 2)
    mate = c + 1 - 2 * parity

    def owned(ref, g, owner):
        return ref.at[g, pl.ds(pl.multiple_of(owner * chans, chans), chans)]

    pair_copies = []
    for g in range(n_dp):
        for m in range(n_ctx // 2):
            slot = g * (n_ctx // 2) + m
            copy = pltpu.make_async_remote_copy(
                src_ref=owned(state_send, g, 2 * m + 1 - parity),
                dst_ref=pair_recv.at[g, m],
                send_sem=pair_sems.at[0, slot],
                recv_sem=pair_sems.at[1, slot],
                device_id={"ctx": mate, "dp": d, "tp": p},
                device_id_type=pl.DeviceIdType.MESH,
            )
            copy.start()
            pair_copies.append(copy)
    xt_copies = [send(xt_ref, xt_recv.at[d], xt_sems, i, o) for i, o in enumerate(across)]
    bt_copies = [send(bt_ref, bt_recv.at[d], bt_sems, i, o) for i, o in enumerate(across)]

    fold = (
        lax.broadcasted_iota(jnp.int32, (dim, chans), 0)
        == lax.rem(lax.broadcasted_iota(jnp.int32, (dim, chans), 1), dim)
    ).astype(F32)
    head_rows = lax.broadcasted_iota(jnp.int32, (heads, chans), 0) == lax.div(
        lax.broadcasted_iota(jnp.int32, (heads, chans), 1), dim
    )

    def flat(value):
        return jnp.sum(jnp.where(head_rows, f32_dot(value, fold), 0.0), axis=0, keepdims=True)

    def spread(value, first):
        count = value.shape[1]
        chosen = (
            lax.broadcasted_iota(jnp.int32, (count, chans), 0)
            == first + lax.div(lax.broadcasted_iota(jnp.int32, (count, chans), 1), dim)
        ).astype(F32)
        return f32_dot(value, chosen)

    owns[1].wait()
    for copy in seg_copies:
        copy.wait_recv()
    decays = []
    for device_at in (c, mate):
        for g in range(n_dp):
            after = jnp.zeros((1, tp_heads), F32)
            for k in range(n_ctx):
                after += jnp.where(k > device_at, seg_recv[k, pl.ds(picks[g], 1), :], 0.0)
            decays.append(jnp.exp(-after))
    decays = jnp.concatenate(decays, axis=0)
    decay_cols = [
        jnp.transpose(spread(decays, (2 * m + parity) * heads)) for m in range(n_ctx // 2)
    ]
    for g in range(n_dp):
        for m in range(n_ctx // 2):
            pair_copies[g * (n_ctx // 2) + m].wait_recv()
            first = pl.multiple_of((2 * m + parity) * chans, chans)
            here = state_send[g, pl.ds(first, chans), :].astype(F32)
            pair_send[g, m] = (
                decay_cols[m][:, g : g + 1] * here
                + decay_cols[m][:, n_dp + g : n_dp + g + 1] * pair_recv[g, m].astype(F32)
            ).astype(BF16)
    state_copies = []
    for a in range(n_ctx // 2):
        for b in range(n_dp):
            if a + b:
                o = (2 * a, b, 0)
                pc, pd, _ = peer(o)
                source = pair_send.at[pd, lax.div(pc, 2)]
                slot = b * (n_ctx // 2) + a
                target = state_recv.at[d, lax.div(c, 2)]
                state_copies.append(send(source, target, state_sems, slot, o))
    state_recv[d, lax.div(c, 2)] = pair_send[d, lax.div(c, 2)]

    for load in smalls:
        load.wait()
    tap_rows = [flat(cxw_ref[k]) for k in range(taps)]
    bias_row = flat(cxb_ref[...])
    gate_row = flat(gg_ref[...])
    dtb_row = spread(dtb_ref[...], 0)
    rate_row = -jnp.exp(spread(alog_ref[...], 0))
    skip_row = spread(skip_ref[...], 0)

    owns[0].wait()
    for copy in emb_copies:
        copy.wait_recv()
    pieces = []
    for i in range(n_ctx * n_tp):
        piece = emb_recv[0, i].astype(F32)
        for g in range(1, n_dp):
            piece += emb_recv[g, i].astype(F32)
        pieces.append(piece)
    embedded = jnp.concatenate(pieces, axis=1)
    scale = lax.rsqrt(jnp.sum(embedded * embedded, axis=1, keepdims=True) / model + epsilon)
    normed = (embedded * scale * gain_ref[...]).astype(BF16)
    loads[1].wait()
    col_send[:, 0:n_cols] = nt_dot(normed, wbc[...])
    col_copies = [send(col_send, col_recv.at[mine], col_sems, i, o) for i, o in enumerate(group)]
    col_recv[mine] = col_send[...]
    loads[2].wait()
    x_rows = nt_dot(normed, wzx[half : 2 * half, :])
    loads[3].wait()
    z_gate = silu(nt_dot(normed, wzx[0:half, :]))

    owns[2].wait()
    owns[3].wait()
    for copy in xt_copies + bt_copies:
        copy.wait_recv()
    holders = [lax.div(dec_ref[d * per + j], per) for j in range(per)]
    places = [lax.rem(dec_ref[d * per + j], per) for j in range(per)]
    plane_rows = lax.broadcasted_iota(jnp.int32, (per, 1), 0)
    for k in range(taps - 1):
        for j in range(per):
            r = k * per + j
            xfull[r : r + 1, :] = flat(xt_recv[holders[j], places[j], k].astype(F32))
            plane = bt_recv[holders[j], k].astype(F32)
            bcfull[r : r + 1, :] = jnp.sum(
                jnp.where(plane_rows == places[j], plane, 0.0), axis=0, keepdims=True
            )
    lead = (taps - 1) * per
    xfull[lead : lead + rows, :] = x_rows
    conv = bias_row
    for k in range(taps):
        conv = conv + tap_rows[k] * xfull[k * per : k * per + rows, :]
    xc = silu(conv)

    for copy in state_copies:
        copy.wait_recv()
    for j in range(per):
        begin = state_recv[holders[j], 0].astype(F32)
        for m in range(1, n_ctx // 2):
            begin += state_recv[holders[j], m].astype(F32)
        start_state[j] = begin

    for copy in col_copies:
        copy.wait_recv()
    wide_pad = jnp.zeros((rows, all_cols - col_send.shape[1]), F32)
    columns = jnp.zeros((rows, all_cols), F32)
    for i in range(n_ctx * n_tp):
        wide = jnp.concatenate([col_recv[i], wide_pad], axis=1)
        columns = columns + (pltpu.roll(wide, n_cols * i, 1) if i else wide)
    bcfull[lead : lead + rows, :] = columns[:, :width]
    conv = cbb_ref[...]
    for k in range(taps):
        conv = conv + cbw_ref[k : k + 1, :] * bcfull[k * per : k * per + rows, :]
    bcc = silu(conv)
    b_all, c_all = bcc[:, :state_n], bcc[:, state_n:]
    head_first = (p * n_ctx + c) * heads
    step_size = softplus(spread(columns[:, width:], head_first) + dtb_row)
    log_keep = step_size * rate_row
    driven = step_size * xc

    row_slot = lax.rem(lax.broadcasted_iota(jnp.int32, (rows, 1), 0), per)
    from_start = jnp.zeros((rows, chans), F32)
    c_low = c_all.astype(BF16)
    for j in range(per):
        from_start += jnp.where(row_slot == j, nt_dot(c_low, start_state[j].astype(BF16)), 0.0)

    def at(value, t):
        return value[t * per : (t + 1) * per]

    total = jnp.zeros((per, chans), F32)
    sums = []
    for t in range(steps):
        total = total + at(log_keep, t)
        sums.append(total)
    for t in range(steps):
        y = jnp.exp(sums[t]) * at(from_start, t) + skip_row * at(xc, t)
        for s in range(t + 1):
            overlap = jnp.sum(at(b_all, s) * at(c_all, t), axis=1, keepdims=True)
            term = at(driven, s) * overlap
            y = y + (term if s == t else jnp.exp(sums[t] - sums[s]) * term)
        gated_ref[t * per : (t + 1) * per, :] = y
    gated = gated_ref[...] * z_gate
    squares = jnp.sum(gated * gated, axis=1, keepdims=True)
    sq_send[...] = jnp.broadcast_to(squares, sq_send.shape)
    sq_copies = [send(sq_send, sq_recv.at[mine], sq_sems, i, o) for i, o in enumerate(group)]
    sq_recv[mine] = sq_send[...]

    loads[4].wait()
    partial = jnp.dot((gated * gate_row).astype(BF16), wout[...], preferred_element_type=F32)
    for i in range(n_ctx * n_tp):
        out_send[i] = partial[:, i * feats : (i + 1) * feats].astype(BF16)
    out_copies = []
    for i, o in enumerate(group):
        pc, _, pp = peer(o)
        out_copies.append(send(out_send.at[pc * n_tp + pp], out_recv.at[mine], out_sems, i, o))
    out_recv[mine] = out_send[mine]

    late = [jnp.exp(sums[-1] - sums[t]) * at(driven, t) for t in range(steps)]
    flat_rows = jnp.concatenate(late + [jnp.exp(sums[-1])] * (rows // per), axis=0)
    tall = jnp.transpose(flat_rows)
    for j in range(per):
        b_own = jnp.where(row_slot == j, b_all, 0.0)
        final_ref[j] = (
            tall[:, rows + j : rows + j + 1] * start_state[j] + f32_dot(tall[:, :rows], b_own)
        )

    final_copy = pltpu.make_async_copy(final_ref, final_hbm, final_sem)
    final_copy.start()

    for copy in sq_copies + out_copies:
        copy.wait_recv()
    total_squares = sq_recv[0]
    mixed = out_recv[0].astype(F32)
    for i in range(1, n_ctx * n_tp):
        total_squares = total_squares + sq_recv[i]
        mixed = mixed + out_recv[i].astype(F32)
    inverse = lax.rsqrt(total_squares[:, 0:1] / (total_heads * dim) + epsilon)
    mixed = mixed * inverse
    for t in range(steps):
        mixed_ref[t] = at(mixed, t).astype(BF16)
    for copy in (
        emb_copies + seg_copies + pair_copies + xt_copies + bt_copies + state_copies + col_copies + sq_copies
        + out_copies
    ):
        copy.wait_send()
    final_copy.wait()


def tail_kernel(mixed_in, final_in, mixed_out, final_out, mixed_buf, final_buf, in_sems, out_sems):
    moves = [(mixed_in, mixed_buf, mixed_out)]
    cuts = 4 if final_in.shape[1] % 32 == 0 else 1
    size = final_in.shape[1] // cuts
    for j in range(final_in.shape[0]):
        for k in range(cuts):
            piece = (j, pl.ds(k * size, size))
            moves.append((final_in.at[piece], final_buf.at[piece], final_out.at[piece]))
    moves = moves[1:] + moves[:1]
    inward = [pltpu.make_async_copy(a, b, in_sems.at[i]) for i, (a, b, _) in enumerate(moves)]
    outward = [pltpu.make_async_copy(b, e, out_sems.at[i]) for i, (_, b, e) in enumerate(moves)]
    for copy in inward:
        copy.start()
    for first, second in zip(inward, outward):
        first.wait()
        second.start()
    for copy in outward:
        copy.wait()


def kernel_device(
    sizes,
    token_ids,
    decode_prompt,
    embedding,
    norm_gain,
    w_zx,
    w_bcdt,
    conv_x_weight,
    conv_x_bias,
    conv_bc_weight,
    conv_bc_bias,
    dt_bias,
    a_log,
    d_skip,
    gate_norm_gain,
    w_out,
    state_parts,
    seg_rate,
    x_tail,
    bc_tail,
):
    n_ctx, n_dp, n_tp, _ = sizes
    steps = token_ids.shape[0]
    slots = decode_prompt.shape[0]
    per = state_parts.shape[1]
    rows = steps * per
    vocab, feats = embedding.shape
    heads, dim, model = w_zx.shape[1:]
    chans = heads * dim
    tp_heads, state_n = state_parts.shape[2], state_parts.shape[4]
    world, ring = n_ctx * n_dp * n_tp, n_ctx * n_tp
    smem = pl.BlockSpec(memory_space=pltpu.SMEM)
    vmem = pl.BlockSpec(memory_space=pltpu.VMEM)
    anywhere = pl.BlockSpec(memory_space=pl.ANY)
    rest = max(1, vocab % ROW_TILE)
    part = pl.pallas_call(
        functools.partial(gather_kernel, steps, slots, n_dp),
        out_shape=jax.ShapeDtypeStruct((n_dp, rows, feats), BF16),
        in_specs=[smem, smem, anywhere],
        out_specs=vmem,
        scratch_shapes=[
            pltpu.VMEM((steps * slots, ROW_TILE, feats), BF16),
            pltpu.VMEM((rest, feats), BF16),
            pltpu.SemaphoreType.DMA((steps * slots,)),
            pltpu.SemaphoreType.DMA,
        ],
        name="gather_rows",
    )(token_ids, decode_prompt, embedding)
    sem = pltpu.SemaphoreType.DMA
    wide = 2 * state_n
    full_rows = -(-(conv_x_weight.shape[0] - 1 + steps) * per // 8) * 8
    smalls = (
        norm_gain[None],
        conv_x_weight,
        conv_x_bias,
        conv_bc_weight,
        conv_bc_bias[None],
        dt_bias[None],
        a_log[None],
        d_skip[None],
        gate_norm_gain,
    )
    bc_planes = jnp.swapaxes(bc_tail, 0, 1)
    outs = (
        jax.ShapeDtypeStruct((steps, per, feats), BF16),
        jax.ShapeDtypeStruct((per, chans, state_n), F32),
    )
    pairs = n_ctx // 2
    mixed, final = pl.pallas_call(
        functools.partial(mixer_kernel, sizes),
        out_shape=outs,
        in_specs=[smem] + [anywhere] * 17,
        out_specs=(vmem, anywhere),
        scratch_shapes=[
            *[pltpu.VMEM(small.shape, small.dtype) for small in smalls],
            pltpu.VMEM((per, chans, state_n), F32),
            pltpu.VMEM((n_dp, pairs, chans, state_n), BF16),
            pltpu.VMEM((n_dp, pairs, chans, state_n), BF16),
            pltpu.VMEM((2 * chans, model), BF16),
            pltpu.VMEM(w_bcdt.shape[::-1], BF16),
            pltpu.VMEM((chans, model), BF16),
            pltpu.VMEM((per, tp_heads * dim, state_n), BF16),
            pltpu.VMEM((n_dp, tp_heads * dim, state_n), BF16),
            pltpu.VMEM((n_dp, pairs, chans, state_n), BF16),
            pltpu.VMEM((n_dp, ring, rows, feats), BF16),
            pltpu.VMEM((n_ctx, per, tp_heads), F32),
            pltpu.VMEM((n_dp,) + x_tail.shape, BF16),
            pltpu.VMEM((n_dp,) + bc_planes.shape, BF16),
            pltpu.VMEM((rows, 128), F32),
            pltpu.VMEM((ring, rows, 128), F32),
            pltpu.VMEM((rows, 128), F32),
            pltpu.VMEM((ring, rows, 128), F32),
            pltpu.VMEM((ring, rows, feats), BF16),
            pltpu.VMEM((ring, rows, feats), BF16),
            pltpu.VMEM((per, chans, state_n), F32),
            pltpu.VMEM((full_rows, chans), F32),
            pltpu.VMEM((full_rows, wide), F32),
            pltpu.VMEM((rows, chans), F32),
            sem((5,)),
            sem((len(smalls),)),
            sem((4,)),
            sem,
            sem((2, n_dp * pairs)),
            sem((2, world)),
            sem((2, n_dp * pairs)),
            sem((2, n_ctx)),
            sem((2, n_dp)),
            sem((2, n_dp)),
            sem((2, ring)),
            sem((2, ring)),
            sem((2, ring)),
        ],
        compiler_params=pltpu.CompilerParams(
            collective_id=0, has_side_effects=True, vmem_limit_bytes=56 * 1024 * 1024
        ),
        name="mixer",
    )(
        decode_prompt,
        part,
        seg_rate,
        x_tail,
        bc_planes,
        *smalls,
        w_zx.reshape(2 * chans, model),
        w_bcdt.T,
        w_out.reshape(chans, model),
        state_parts.reshape(per, tp_heads * dim, state_n),
    )
    mixed, final = pl.pallas_call(
        tail_kernel,
        out_shape=outs,
        in_specs=[anywhere] * 2,
        out_specs=(anywhere, anywhere),
        scratch_shapes=[
            pltpu.VMEM(outs[0].shape, BF16),
            pltpu.VMEM(outs[1].shape, F32),
            sem((4 * per + 1,)),
            sem((4 * per + 1,)),
        ],
        name="tail",
    )(mixed, final)
    return mixed, final.reshape(per, heads, dim, state_n)


def choose_device(sizes, *args):
    embedding, w_zx, w_bcdt = args[2], args[4], args[5]
    heads, dim = w_zx.shape[1:3]
    fits = (
        embedding.shape[1] % 128 == 0
        and sizes[0] % 2 == 0
        and (heads * dim) % 128 == 0
        and w_bcdt.shape[1] <= 128
        and embedding.shape[0] >= ROW_TILE
    )
    if fits:
        return kernel_device(sizes, *args)
    return per_device(*args)


def solution(mesh):
    sizes = (mesh.shape["ctx"], mesh.shape["dp"], mesh.shape["tp"], HEADS)
    return jax.shard_map(
        functools.partial(choose_device, sizes),
        mesh=mesh,
        in_specs=(
            P(),
            P(),
            P("dp", ("ctx", "tp")),
            P(),
            P(None, ("tp", "ctx"), None, None),
            P(None, ("ctx", "tp")),
            P(None, ("tp", "ctx"), None),
            P(("tp", "ctx"), None),
            P(),
            P(),
            P(("tp", "ctx")),
            P(("tp", "ctx")),
            P(("tp", "ctx")),
            P(("tp", "ctx"), None),
            P(("tp", "ctx"), None, None),
            P("ctx", "dp", "tp", None, None),
            P("ctx", "dp", "tp"),
            P("dp", None, ("tp", "ctx"), None),
            P("dp", None, None),
        ),
        out_specs=(P(None, "dp", ("ctx", "tp")), P("dp", ("tp", "ctx"), None, None)),
        check_vma=False,
    )
```

```python
import functools

import jax
import jax.numpy as jnp
from jax import lax
from jax.experimental import pallas as pl
from jax.experimental.pallas import tpu as pltpu
from jax.sharding import PartitionSpec as P

HEADS = 128
HEAD_DIM = 64


epsilon = 1e-05


def entering(shard, axis, combine, identity):
    count, here = (lax.axis_size(axis), lax.axis_index(axis))
    everything = lax.all_gather(shard, axis)
    start = jnp.broadcast_to(jnp.asarray(identity, shard.dtype), shard.shape)

    def step(k, before):
        at = count - 1 - k
        reached = at > here
        new = combine(before, everything[at])
        return jnp.where(reached, new, before)

    return lax.fori_loop(0, count, step, start)


def rms_scale(values, gain):
    return values * lax.rsqrt(jnp.mean(values * values, axis=-1, keepdims=True) + epsilon) * gain


def select_rows(picker, values):
    return jnp.tensordot(picker, values, axes=1, precision=lax.Precision.HIGHEST)


def add_rates(earlier, later_one):
    return earlier + later_one


def per_device(
    token_ids,
    decode_prompt,
    embedding,
    norm_gain,
    w_zx,
    w_bcdt,
    conv_x_weight,
    conv_x_bias,
    conv_bc_weight,
    conv_bc_bias,
    dt_bias,
    a_log,
    d_skip,
    gate_norm_gain,
    w_out,
    state_parts,
    seg_rate,
    x_tail,
    bc_tail,
):
    group = lax.axis_index("dp")
    local_count = state_parts.shape[1]
    slot_count = decode_prompt.shape[0]
    head_count = w_zx.shape[1]
    state_width = conv_bc_bias.shape[0] // 2
    after_rates = entering(seg_rate, "ctx", add_rates, jnp.zeros_like(seg_rate))
    seg_weight = jnp.exp(-after_rates[0])
    scaled = seg_weight[:, :, None, None] * state_parts[0].astype(jnp.float32)
    channel_sums = lax.psum_scatter(
        scaled.astype(jnp.bfloat16), "ctx", scatter_dimension=2, tiled=True
    ).astype(jnp.float32)
    combined = lax.all_to_all(
        channel_sums.astype(jnp.bfloat16), "ctx", split_axis=1, concat_axis=2, tiled=True
    ).astype(channel_sums.dtype)
    tails_x = x_tail.astype(jnp.float32)
    tails_bc = bc_tail.astype(jnp.float32)
    own_slots = lax.dynamic_slice_in_dim(decode_prompt, group * local_count, local_count)
    prompt_ids = jnp.arange(slot_count, dtype=jnp.int32)
    every_state, every_x, every_bc = (
        lax.all_gather(combined.astype(jnp.bfloat16), "dp", axis=0, tiled=True).astype(
            combined.dtype
        ),
        lax.all_gather(tails_x.astype(jnp.bfloat16), "dp", axis=0, tiled=True).astype(
            tails_x.dtype
        ),
        lax.all_gather(tails_bc.astype(jnp.bfloat16), "dp", axis=0, tiled=True).astype(
            tails_bc.dtype
        ),
    )
    picker = (own_slots[:, None] == prompt_ids[None, :]).astype(jnp.float32)
    ssm_state = select_rows(picker, every_state)
    x_window = select_rows(picker, every_x)
    bc_window = select_rows(picker, every_bc)
    vocab_rows = embedding.shape[0]
    holder = (decode_prompt[:, None] == prompt_ids[None, :]).astype(jnp.int32)
    slot_tokens = jnp.sum(token_ids[:, None, :] * holder[None], axis=2)
    offset_tokens = slot_tokens - group * vocab_rows
    inside = (offset_tokens >= 0) & (offset_tokens < vocab_rows)
    looked = jnp.take(embedding, jnp.clip(offset_tokens, 0, vocab_rows - 1), axis=0)
    partial_rows = jnp.where(inside[..., None], looked.astype(jnp.float32), 0.0)
    own_rows = lax.psum_scatter(
        partial_rows.astype(jnp.bfloat16), "dp", scatter_dimension=1, tiled=True
    )
    embedded = lax.all_gather(own_rows, ("ctx", "tp"), axis=2, tiled=True)
    steps_count = embedded.shape[0]
    flat_rows = embedded.reshape(-1, embedded.shape[2]).astype(jnp.float32)
    normed = rms_scale(flat_rows, norm_gain).astype(jnp.bfloat16)
    projected = jnp.einsum("rd,khed->krhe", normed, w_zx, preferred_element_type=jnp.float32)
    projected = projected.reshape(
        2, steps_count, local_count, projected.shape[2], projected.shape[3]
    )
    columns = lax.all_gather(
        jnp.dot(normed, w_bcdt, preferred_element_type=jnp.float32),
        ("ctx", "tp"),
        axis=1,
        tiled=True,
    )
    columns = columns.reshape(steps_count, local_count, -1)
    head_block = lax.axis_index("tp") * lax.axis_size("ctx") + lax.axis_index("ctx")
    head_start = 2 * state_width + head_block * head_count
    dt_raw = lax.dynamic_slice_in_dim(columns, head_start, head_count, 2)
    decay_rate = -jnp.exp(a_log)
    gated_steps = []
    for moment in range(steps_count):
        x_window = jnp.concatenate([x_window, projected[1, moment][:, None]], axis=1)
        bc_window = jnp.concatenate(
            [bc_window, columns[moment, :, None, : 2 * state_width]], axis=1
        )
        x_conv = jax.nn.silu(jnp.einsum("pkhe,khe->phe", x_window, conv_x_weight) + conv_x_bias)
        bc_conv = jax.nn.silu(jnp.einsum("pkn,kn->pn", bc_window, conv_bc_weight) + conv_bc_bias)
        step_size = jax.nn.softplus(dt_raw[moment] + dt_bias)
        retain = jnp.exp(step_size * decay_rate)
        ssm_state = (
            retain[:, :, None, None] * ssm_state
            + (step_size[:, :, None] * x_conv)[:, :, :, None] * bc_conv[:, None, None, :state_width]
        )
        output = (
            jnp.einsum("phen,pn->phe", ssm_state, bc_conv[:, state_width:])
            + d_skip[None, :, None] * x_conv
        )
        gated_steps.append(output * jax.nn.silu(projected[0, moment]))
        x_window = x_window[:, 1:]
        bc_window = bc_window[:, 1:]
    gated_all = jnp.stack(gated_steps)
    local_squares = jnp.sum(gated_all * gated_all, axis=(2, 3))
    total_squares = lax.psum(local_squares, ("ctx", "tp"))
    inverse = lax.rsqrt(total_squares / (HEADS * HEAD_DIM) + epsilon)
    normed_out = (gated_all * inverse[:, :, None, None] * gate_norm_gain).astype(jnp.bfloat16)
    partial_out = jnp.einsum("tphe,hed->tpd", normed_out, w_out, preferred_element_type=jnp.float32)
    outer_sum = lax.psum_scatter(
        partial_out.astype(jnp.bfloat16), "ctx", scatter_dimension=2, tiled=True
    ).astype(jnp.float32)
    mixed = lax.psum_scatter(outer_sum, "tp", scatter_dimension=2, tiled=True)
    return (mixed.astype(jnp.bfloat16), ssm_state)


HI = lax.Precision.HIGHEST
F32 = jnp.float32
BF16 = jnp.bfloat16


def f32_dot(a, b):
    return jnp.dot(a, b, precision=HI, preferred_element_type=F32)


def nt_dot(a, b):
    return lax.dot_general(a, b, (((1,), (1,)), ((), ())), preferred_element_type=F32)


def silu(v):
    return v / (1.0 + jnp.exp(-v))


def softplus(v):
    return jnp.maximum(v, 0.0) + jnp.log1p(jnp.exp(-jnp.abs(v)))


ROW_TILE = 16


def gather_kernel(steps, slots, groups, tok_ref, dec_ref, emb_ref, out_ref, buf, tail, sems, tail_sem):
    vocab = emb_ref.shape[0]
    whole = vocab // ROW_TILE * ROW_TILE
    base = lax.axis_index("dp") * vocab
    per_group = slots // groups
    tail_copy = None
    if whole < vocab:
        tail_copy = pltpu.make_async_copy(emb_ref.at[pl.ds(whole, vocab - whole)], tail, tail_sem)
        tail_copy.start()
    copies = []
    where = []
    for s in range(slots):
        q = dec_ref[s]
        for t in range(steps):
            row = tok_ref[t, q] - base
            clipped = jnp.clip(row, 0, vocab - 1)
            start = jnp.minimum(clipped // ROW_TILE * ROW_TILE, whole - ROW_TILE)
            start = pl.multiple_of(start, ROW_TILE)
            i = s * steps + t
            copy = pltpu.make_async_copy(emb_ref.at[pl.ds(start, ROW_TILE)], buf.at[i], sems.at[i])
            copy.start()
            copies.append(copy)
            where.append((row, start))
    if tail_copy is not None:
        tail_copy.wait()
    for copy in copies:
        copy.wait()
    rows = lax.broadcasted_iota(jnp.int32, (ROW_TILE, 1), 0)
    for g in range(groups):
        picked = []
        for t in range(steps):
            for j in range(per_group):
                i = (g * per_group + j) * steps + t
                row, start = where[i]
                value = jnp.sum(
                    jnp.where(rows == row - start, buf[i].astype(F32), 0.0), axis=0, keepdims=True
                )
                if tail_copy is not None:
                    trows = lax.broadcasted_iota(jnp.int32, (vocab - whole, 1), 0)
                    value += jnp.sum(
                        jnp.where(trows == row - whole, tail[...].astype(F32), 0.0),
                        axis=0,
                        keepdims=True,
                    )
                picked.append(value)
        out_ref[g] = jnp.concatenate(picked, axis=0).astype(BF16)


def mixer_kernel(
    sizes,
    dec_ref,
    part_ref,
    seg_ref,
    xt_ref,
    bt_ref,
    gain_hbm,
    cxw_hbm,
    cxb_hbm,
    cbw_hbm,
    cbb_hbm,
    dtb_hbm,
    alog_hbm,
    skip_hbm,
    gg_hbm,
    wzx_hbm,
    wbc_hbm,
    wout_hbm,
    state_hbm,
    mixed_ref,
    final_hbm,
    gain_ref,
    cxw_ref,
    cxb_ref,
    cbw_ref,
    cbb_ref,
    dtb_ref,
    alog_ref,
    skip_ref,
    gg_ref,
    final_ref,
    pair_recv,
    pair_send,
    wzx,
    wbc,
    wout,
    state_in,
    state_send,
    state_recv,
    emb_recv,
    seg_recv,
    xt_recv,
    bt_recv,
    col_send,
    col_recv,
    sq_send,
    sq_recv,
    out_send,
    out_recv,
    start_state,
    xfull,
    bcfull,
    gated_ref,
    load_sems,
    small_sems,
    own_sems,
    final_sem,
    pair_sems,
    seg_mate,
    seg_own,
    emb_sems,
    state_sems,
    seg_sems,
    xt_sems,
    bt_sems,
    col_sems,
    sq_sems,
    out_sems,
):
    n_ctx, n_dp, n_tp, total_heads = sizes
    c, d, p = lax.axis_index("ctx"), lax.axis_index("dp"), lax.axis_index("tp")
    mine = c * n_tp + p
    steps, per, feats = mixed_ref.shape
    rows = steps * per
    heads, dim = cxb_ref.shape
    chans = heads * dim
    width = cbb_ref.shape[1]
    state_n = width // 2
    taps = cxw_ref.shape[0]
    model = gain_ref.shape[1]
    tp_heads = seg_ref.shape[-1]
    n_cols = wbc_hbm.shape[0]
    all_cols = n_cols * n_ctx * n_tp

    def peer(offset):
        dc, dd, dt = offset
        return lax.rem(c + dc, n_ctx), lax.rem(d + dd, n_dp), lax.rem(p + dt, n_tp)

    def device(offset):
        a, b, e = peer(offset)
        return {"ctx": a, "dp": b, "tp": e}

    everyone = [
        (a, b, e) for a in range(n_ctx) for b in range(n_dp) for e in range(n_tp) if a + b + e
    ]
    everyone.sort(key=lambda o: -(min(o[2], n_tp - o[2]) * 4 + o[1] * 2 + o[0]))
    group = [o for o in everyone if o[1] == 0]
    routed = [o for o in everyone if o[2] == 0]
    across = [o for o in everyone if o[0] == 0 and o[2] == 0]

    barrier = pltpu.get_barrier_semaphore()
    for o in everyone:
        pl.semaphore_signal(
            barrier, inc=1, device_id=device(o), device_id_type=pl.DeviceIdType.MESH
        )

    loads = []
    half = wzx_hbm.shape[0] // 2
    pairs = (
        (state_hbm, state_in),
        (wbc_hbm, wbc),
        (wzx_hbm.at[pl.ds(half, half)], wzx.at[pl.ds(half, half)]),
        (wzx_hbm.at[pl.ds(0, half)], wzx.at[pl.ds(0, half)]),
        (wout_hbm, wout),
    )
    for i, (source, target) in enumerate(pairs):
        load = pltpu.make_async_copy(source, target, load_sems.at[i])
        load.start()
        loads.append(load)

    small_pairs = (
        (gain_hbm, gain_ref),
        (cxw_hbm, cxw_ref),
        (cxb_hbm, cxb_ref),
        (cbw_hbm, cbw_ref),
        (cbb_hbm, cbb_ref),
        (dtb_hbm, dtb_ref),
        (alog_hbm, alog_ref),
        (skip_hbm, skip_ref),
        (gg_hbm, gg_ref),
    )
    smalls = []
    for i, (source, target) in enumerate(small_pairs):
        load = pltpu.make_async_copy(source, target, small_sems.at[i])
        load.start()
        smalls.append(load)
    owns = []
    for source, target in (
        (part_ref.at[d], emb_recv.at[d, mine]),
        (seg_ref.at[0], seg_recv.at[d, c]),
        (xt_ref, xt_recv.at[d]),
        (bt_ref, bt_recv.at[d]),
        (seg_ref.at[0], seg_own),
    ):
        load = pltpu.make_async_copy(source, target, own_sems.at[len(owns)])
        load.start()
        owns.append(load)

    def send(source, target, sems, slot, offset):
        copy = pltpu.make_async_remote_copy(
            src_ref=source,
            dst_ref=target,
            send_sem=sems.at[0, slot],
            recv_sem=sems.at[1, slot],
            device_id=device(offset),
            device_id_type=pl.DeviceIdType.MESH,
        )
        copy.start()
        return copy

    loads[0].wait()
    picks = []
    for b in range(n_dp):
        target_group = lax.rem(d + b, n_dp)
        pick = jnp.int32(0)
        for j in range(per):
            local = dec_ref[target_group * per + j] - d * per
            pick += jnp.where((local >= 0) & (local < per), local, 0)
        state_send[b] = state_in[pick]
        picks.append(pick)

    col_send[...] = jnp.zeros_like(col_send)

    pl.semaphore_wait(barrier, len(everyone))

    emb_copies = [
        send(part_ref.at[peer(o)[1]], emb_recv.at[d, mine], emb_sems, i, o)
        for i, o in enumerate(everyone)
    ]
    parity = lax.rem(c, 2)
    mate = c + 1 - 2 * parity
    blocks = [(a, b) for a in reversed(range(n_ctx // 2)) for b in reversed(range(n_dp))]

    def to_mate(source, target, slot):
        copy = pltpu.make_async_remote_copy(
            src_ref=source,
            dst_ref=target,
            send_sem=pair_sems.at[0, slot],
            recv_sem=pair_sems.at[1, slot],
            device_id={"ctx": mate, "dp": d, "tp": p},
            device_id_type=pl.DeviceIdType.MESH,
        )
        copy.start()
        return copy

    mate_copy = to_mate(seg_ref.at[0], seg_mate, len(blocks))
    pair_copies = []
    for slot, (a, b) in enumerate(blocks):
        first = pl.multiple_of(lax.rem(mate + 2 * a, n_ctx) * chans, chans)
        source = state_send.at[b, pl.ds(first, chans)]
        pair_copies.append(to_mate(source, pair_recv.at[b, a], slot))
    pair_copies.append(mate_copy)
    seg_copies = [send(seg_ref.at[0], seg_recv.at[d, c], seg_sems, i, o) for i, o in enumerate(routed)]
    xt_copies = [send(xt_ref, xt_recv.at[d], xt_sems, i, o) for i, o in enumerate(across)]
    bt_copies = [send(bt_ref, bt_recv.at[d], bt_sems, i, o) for i, o in enumerate(across)]

    fold = (
        lax.broadcasted_iota(jnp.int32, (dim, chans), 0)
        == lax.rem(lax.broadcasted_iota(jnp.int32, (dim, chans), 1), dim)
    ).astype(F32)
    head_rows = lax.broadcasted_iota(jnp.int32, (heads, chans), 0) == lax.div(
        lax.broadcasted_iota(jnp.int32, (heads, chans), 1), dim
    )

    def flat(value):
        return jnp.sum(jnp.where(head_rows, f32_dot(value, fold), 0.0), axis=0, keepdims=True)

    def spread(value, first):
        count = value.shape[1]
        chosen = (
            lax.broadcasted_iota(jnp.int32, (count, chans), 0)
            == first + lax.div(lax.broadcasted_iota(jnp.int32, (count, chans), 1), dim)
        ).astype(F32)
        return f32_dot(value, chosen)

    owns[4].wait()
    mate_copy.wait_recv()
    shrink = []
    for b in range(n_dp):
        row = pl.ds(picks[b], 1)
        shrink.append(jnp.exp(-jnp.where(parity == 0, seg_mate[row, :], seg_own[row, :])))
    ones = [jnp.ones((1, tp_heads), F32)] * n_dp
    shrink = jnp.concatenate(shrink + ones, axis=0)
    shrink_cols = [
        jnp.transpose(spread(shrink, lax.rem(c + 2 * a, n_ctx) * heads)) for a in range(n_ctx // 2)
    ]
    state_copies = []
    for slot, (a, b) in enumerate(blocks):
        pair_copies[slot].wait_recv()
        first = pl.multiple_of(lax.rem(c + 2 * a, n_ctx) * chans, chans)
        here = state_send[b, pl.ds(first, chans), :].astype(F32)
        there = pair_recv[b, a].astype(F32)
        factor = shrink_cols[a][:, b : b + 1]
        even = jnp.where(parity == 0, here, there)
        odd = jnp.where(parity == 0, there, here)
        added = (factor * even + odd).astype(BF16)
        target = state_recv.at[d, lax.div(c, 2)]
        if a + b:
            pair_send[b, a] = added
            state_copies.append(send(pair_send.at[b, a], target, state_sems, slot, (2 * a, b, 0)))
        else:
            state_recv[d, lax.div(c, 2)] = added

    for load in smalls:
        load.wait()
    tap_rows = [flat(cxw_ref[k]) for k in range(taps)]
    bias_row = flat(cxb_ref[...])
    gate_row = flat(gg_ref[...])
    dtb_row = spread(dtb_ref[...], 0)
    rate_row = -jnp.exp(spread(alog_ref[...], 0))
    skip_row = spread(skip_ref[...], 0)

    owns[0].wait()
    for copy in emb_copies:
        copy.wait_recv()
    pieces = []
    for i in range(n_ctx * n_tp):
        piece = emb_recv[0, i].astype(F32)
        for g in range(1, n_dp):
            piece += emb_recv[g, i].astype(F32)
        pieces.append(piece)
    embedded = jnp.concatenate(pieces, axis=1)
    scale = lax.rsqrt(jnp.sum(embedded * embedded, axis=1, keepdims=True) / model + epsilon)
    normed = (embedded * scale * gain_ref[...]).astype(BF16)
    loads[1].wait()
    col_send[:, 0:n_cols] = nt_dot(normed, wbc[...])
    col_copies = [send(col_send, col_recv.at[mine], col_sems, i, o) for i, o in enumerate(group)]
    col_recv[mine] = col_send[...]
    loads[2].wait()
    x_rows = nt_dot(normed, wzx[half : 2 * half, :])
    loads[3].wait()
    z_gate = silu(nt_dot(normed, wzx[0:half, :]))

    owns[2].wait()
    owns[3].wait()
    for copy in xt_copies + bt_copies:
        copy.wait_recv()
    holders = [lax.div(dec_ref[d * per + j], per) for j in range(per)]
    places = [lax.rem(dec_ref[d * per + j], per) for j in range(per)]
    plane_rows = lax.broadcasted_iota(jnp.int32, (per, 1), 0)
    for k in range(taps - 1):
        for j in range(per):
            r = k * per + j
            xfull[r : r + 1, :] = flat(xt_recv[holders[j], places[j], k].astype(F32))
            plane = bt_recv[holders[j], k].astype(F32)
            bcfull[r : r + 1, :] = jnp.sum(
                jnp.where(plane_rows == places[j], plane, 0.0), axis=0, keepdims=True
            )
    lead = (taps - 1) * per
    xfull[lead : lead + rows, :] = x_rows
    conv = bias_row
    for k in range(taps):
        conv = conv + tap_rows[k] * xfull[k * per : k * per + rows, :]
    xc = silu(conv)

    owns[1].wait()
    for copy in seg_copies:
        copy.wait_recv()
    weights = []
    for j in range(per):
        after = jnp.zeros((1, tp_heads), F32)
        ordered = []
        row = pl.ds(places[j], 1)
        for m in reversed(range(n_ctx // 2)):
            ordered.append(jnp.exp(-after))
            for k in (2 * m + 1, 2 * m):
                after = after + seg_recv[holders[j], k, row, :]
        weights.extend(reversed(ordered))
    weight_cols = jnp.transpose(spread(jnp.concatenate(weights, axis=0), c * heads))
    for copy in state_copies:
        copy.wait_recv()
    for j in range(per):
        begin = None
        for m in range(n_ctx // 2):
            r = j * (n_ctx // 2) + m
            term = weight_cols[:, r : r + 1] * state_recv[holders[j], m].astype(F32)
            begin = term if begin is None else begin + term
        start_state[j] = begin

    for copy in col_copies:
        copy.wait_recv()
    wide_pad = jnp.zeros((rows, all_cols - col_send.shape[1]), F32)
    columns = jnp.zeros((rows, all_cols), F32)
    for i in range(n_ctx * n_tp):
        wide = jnp.concatenate([col_recv[i], wide_pad], axis=1)
        columns = columns + (pltpu.roll(wide, n_cols * i, 1) if i else wide)
    bcfull[lead : lead + rows, :] = columns[:, :width]
    conv = cbb_ref[...]
    for k in range(taps):
        conv = conv + cbw_ref[k : k + 1, :] * bcfull[k * per : k * per + rows, :]
    bcc = silu(conv)
    b_all, c_all = bcc[:, :state_n], bcc[:, state_n:]
    head_first = (p * n_ctx + c) * heads
    step_size = softplus(spread(columns[:, width:], head_first) + dtb_row)
    log_keep = step_size * rate_row
    driven = step_size * xc

    row_slot = lax.rem(lax.broadcasted_iota(jnp.int32, (rows, 1), 0), per)
    from_start = jnp.zeros((rows, chans), F32)
    c_low = c_all.astype(BF16)
    for j in range(per):
        from_start += jnp.where(row_slot == j, nt_dot(c_low, start_state[j].astype(BF16)), 0.0)

    def at(value, t):
        return value[t * per : (t + 1) * per]

    total = jnp.zeros((per, chans), F32)
    sums = []
    for t in range(steps):
        total = total + at(log_keep, t)
        sums.append(total)
    for t in range(steps):
        y = jnp.exp(sums[t]) * at(from_start, t) + skip_row * at(xc, t)
        for s in range(t + 1):
            overlap = jnp.sum(at(b_all, s) * at(c_all, t), axis=1, keepdims=True)
            term = at(driven, s) * overlap
            y = y + (term if s == t else jnp.exp(sums[t] - sums[s]) * term)
        gated_ref[t * per : (t + 1) * per, :] = y
    gated = gated_ref[...] * z_gate
    squares = jnp.sum(gated * gated, axis=1, keepdims=True)
    sq_send[...] = jnp.broadcast_to(squares, sq_send.shape)
    sq_copies = [send(sq_send, sq_recv.at[mine], sq_sems, i, o) for i, o in enumerate(group)]
    sq_recv[mine] = sq_send[...]

    loads[4].wait()
    partial = jnp.dot((gated * gate_row).astype(BF16), wout[...], preferred_element_type=F32)
    for i in range(n_ctx * n_tp):
        out_send[i] = partial[:, i * feats : (i + 1) * feats].astype(BF16)
    out_copies = []
    for i, o in enumerate(group):
        pc, _, pp = peer(o)
        out_copies.append(send(out_send.at[pc * n_tp + pp], out_recv.at[mine], out_sems, i, o))
    out_recv[mine] = out_send[mine]

    late = [jnp.exp(sums[-1] - sums[t]) * at(driven, t) for t in range(steps)]
    flat_rows = jnp.concatenate(late + [jnp.exp(sums[-1])] * (rows // per), axis=0)
    tall = jnp.transpose(flat_rows)
    for j in range(per):
        b_own = jnp.where(row_slot == j, b_all, 0.0)
        final_ref[j] = (
            tall[:, rows + j : rows + j + 1] * start_state[j] + f32_dot(tall[:, :rows], b_own)
        )

    final_copy = pltpu.make_async_copy(final_ref, final_hbm, final_sem)
    final_copy.start()

    for copy in sq_copies + out_copies:
        copy.wait_recv()
    total_squares = sq_recv[0]
    mixed = out_recv[0].astype(F32)
    for i in range(1, n_ctx * n_tp):
        total_squares = total_squares + sq_recv[i]
        mixed = mixed + out_recv[i].astype(F32)
    inverse = lax.rsqrt(total_squares[:, 0:1] / (total_heads * dim) + epsilon)
    mixed = mixed * inverse
    for t in range(steps):
        mixed_ref[t] = at(mixed, t).astype(BF16)
    for copy in (
        emb_copies + seg_copies + pair_copies + xt_copies + bt_copies + state_copies + col_copies + sq_copies
        + out_copies
    ):
        copy.wait_send()
    final_copy.wait()


def tail_kernel(mixed_in, final_in, mixed_out, final_out, mixed_buf, final_buf, in_sems, out_sems):
    moves = [(mixed_in, mixed_buf, mixed_out)]
    cuts = 4 if final_in.shape[1] % 32 == 0 else 1
    size = final_in.shape[1] // cuts
    for j in range(final_in.shape[0]):
        for k in range(cuts):
            piece = (j, pl.ds(k * size, size))
            moves.append((final_in.at[piece], final_buf.at[piece], final_out.at[piece]))
    moves = moves[1:] + moves[:1]
    inward = [pltpu.make_async_copy(a, b, in_sems.at[i]) for i, (a, b, _) in enumerate(moves)]
    outward = [pltpu.make_async_copy(b, e, out_sems.at[i]) for i, (_, b, e) in enumerate(moves)]
    for copy in inward:
        copy.start()
    for first, second in zip(inward, outward):
        first.wait()
        second.start()
    for copy in outward:
        copy.wait()


def kernel_device(
    sizes,
    token_ids,
    decode_prompt,
    embedding,
    norm_gain,
    w_zx,
    w_bcdt,
    conv_x_weight,
    conv_x_bias,
    conv_bc_weight,
    conv_bc_bias,
    dt_bias,
    a_log,
    d_skip,
    gate_norm_gain,
    w_out,
    state_parts,
    seg_rate,
    x_tail,
    bc_tail,
):
    n_ctx, n_dp, n_tp, _ = sizes
    steps = token_ids.shape[0]
    slots = decode_prompt.shape[0]
    per = state_parts.shape[1]
    rows = steps * per
    vocab, feats = embedding.shape
    heads, dim, model = w_zx.shape[1:]
    chans = heads * dim
    tp_heads, state_n = state_parts.shape[2], state_parts.shape[4]
    world, ring = n_ctx * n_dp * n_tp, n_ctx * n_tp
    smem = pl.BlockSpec(memory_space=pltpu.SMEM)
    vmem = pl.BlockSpec(memory_space=pltpu.VMEM)
    anywhere = pl.BlockSpec(memory_space=pl.ANY)
    rest = max(1, vocab % ROW_TILE)
    part = pl.pallas_call(
        functools.partial(gather_kernel, steps, slots, n_dp),
        out_shape=jax.ShapeDtypeStruct((n_dp, rows, feats), BF16),
        in_specs=[smem, smem, anywhere],
        out_specs=vmem,
        scratch_shapes=[
            pltpu.VMEM((steps * slots, ROW_TILE, feats), BF16),
            pltpu.VMEM((rest, feats), BF16),
            pltpu.SemaphoreType.DMA((steps * slots,)),
            pltpu.SemaphoreType.DMA,
        ],
        name="gather_rows",
    )(token_ids, decode_prompt, embedding)
    sem = pltpu.SemaphoreType.DMA
    wide = 2 * state_n
    full_rows = -(-(conv_x_weight.shape[0] - 1 + steps) * per // 8) * 8
    smalls = (
        norm_gain[None],
        conv_x_weight,
        conv_x_bias,
        conv_bc_weight,
        conv_bc_bias[None],
        dt_bias[None],
        a_log[None],
        d_skip[None],
        gate_norm_gain,
    )
    bc_planes = jnp.swapaxes(bc_tail, 0, 1)
    outs = (
        jax.ShapeDtypeStruct((steps, per, feats), BF16),
        jax.ShapeDtypeStruct((per, chans, state_n), F32),
    )
    pairs = n_ctx // 2
    mixed, final = pl.pallas_call(
        functools.partial(mixer_kernel, sizes),
        out_shape=outs,
        in_specs=[smem] + [anywhere] * 17,
        out_specs=(vmem, anywhere),
        scratch_shapes=[
            *[pltpu.VMEM(small.shape, small.dtype) for small in smalls],
            pltpu.VMEM((per, chans, state_n), F32),
            pltpu.VMEM((n_dp, pairs, chans, state_n), BF16),
            pltpu.VMEM((n_dp, pairs, chans, state_n), BF16),
            pltpu.VMEM((2 * chans, model), BF16),
            pltpu.VMEM(w_bcdt.shape[::-1], BF16),
            pltpu.VMEM((chans, model), BF16),
            pltpu.VMEM((per, tp_heads * dim, state_n), BF16),
            pltpu.VMEM((n_dp, tp_heads * dim, state_n), BF16),
            pltpu.VMEM((n_dp, pairs, chans, state_n), BF16),
            pltpu.VMEM((n_dp, ring, rows, feats), BF16),
            pltpu.VMEM((n_dp, n_ctx, per, tp_heads), F32),
            pltpu.VMEM((n_dp,) + x_tail.shape, BF16),
            pltpu.VMEM((n_dp,) + bc_planes.shape, BF16),
            pltpu.VMEM((rows, 128), F32),
            pltpu.VMEM((ring, rows, 128), F32),
            pltpu.VMEM((rows, 128), F32),
            pltpu.VMEM((ring, rows, 128), F32),
            pltpu.VMEM((ring, rows, feats), BF16),
            pltpu.VMEM((ring, rows, feats), BF16),
            pltpu.VMEM((per, chans, state_n), F32),
            pltpu.VMEM((full_rows, chans), F32),
            pltpu.VMEM((full_rows, wide), F32),
            pltpu.VMEM((rows, chans), F32),
            sem((5,)),
            sem((len(smalls),)),
            sem((5,)),
            sem,
            sem((2, n_dp * pairs + 1)),
            pltpu.VMEM((per, tp_heads), F32),
            pltpu.VMEM((per, tp_heads), F32),
            sem((2, world)),
            sem((2, n_dp * pairs)),
            sem((2, n_ctx * n_dp)),
            sem((2, n_dp)),
            sem((2, n_dp)),
            sem((2, ring)),
            sem((2, ring)),
            sem((2, ring)),
        ],
        compiler_params=pltpu.CompilerParams(
            collective_id=0, has_side_effects=True, vmem_limit_bytes=56 * 1024 * 1024
        ),
        name="mixer",
    )(
        decode_prompt,
        part,
        seg_rate,
        x_tail,
        bc_planes,
        *smalls,
        w_zx.reshape(2 * chans, model),
        w_bcdt.T,
        w_out.reshape(chans, model),
        state_parts.reshape(per, tp_heads * dim, state_n),
    )
    mixed, final = pl.pallas_call(
        tail_kernel,
        out_shape=outs,
        in_specs=[anywhere] * 2,
        out_specs=(anywhere, anywhere),
        scratch_shapes=[
            pltpu.VMEM(outs[0].shape, BF16),
            pltpu.VMEM(outs[1].shape, F32),
            sem((4 * per + 1,)),
            sem((4 * per + 1,)),
        ],
        name="tail",
    )(mixed, final)
    return mixed, final.reshape(per, heads, dim, state_n)


def choose_device(sizes, *args):
    embedding, w_zx, w_bcdt = args[2], args[4], args[5]
    heads, dim = w_zx.shape[1:3]
    fits = (
        embedding.shape[1] % 128 == 0
        and sizes[0] % 2 == 0
        and (heads * dim) % 128 == 0
        and w_bcdt.shape[1] <= 128
        and embedding.shape[0] >= ROW_TILE
    )
    if fits:
        return kernel_device(sizes, *args)
    return per_device(*args)


def solution(mesh):
    sizes = (mesh.shape["ctx"], mesh.shape["dp"], mesh.shape["tp"], HEADS)
    return jax.shard_map(
        functools.partial(choose_device, sizes),
        mesh=mesh,
        in_specs=(
            P(),
            P(),
            P("dp", ("ctx", "tp")),
            P(),
            P(None, ("tp", "ctx"), None, None),
            P(None, ("ctx", "tp")),
            P(None, ("tp", "ctx"), None),
            P(("tp", "ctx"), None),
            P(),
            P(),
            P(("tp", "ctx")),
            P(("tp", "ctx")),
            P(("tp", "ctx")),
            P(("tp", "ctx"), None),
            P(("tp", "ctx"), None, None),
            P("ctx", "dp", "tp", None, None),
            P("ctx", "dp", "tp"),
            P("dp", None, ("tp", "ctx"), None),
            P("dp", None, None),
        ),
        out_specs=(P(None, "dp", ("ctx", "tp")), P("dp", ("tp", "ctx"), None, None)),
        check_vma=False,
    )
```
